128 devices in a mesh: client: 16 (over x, z), shard: 8 (over y, core).
Axes of the slice: x: 4, y: 4, z: 4, core: 2. Of those that a mesh axis runs over, the one named last changes fastest.
Arguments:
- delta: bfloat16 [16, 4096, 14336], P('client', 'shard'), may hold values from -750 to 750
- start_coeffs: bfloat16 [14336, 64], replicated, may hold values from -0.046875 to 0.046875
- noise_p: float32 [2, 4096, 64], P(None, 'shard'), may hold values from -6 to 6
- noise_q: float32 [2, 14336, 64], P(None, 'shard'), may hold values from -6 to 6
Outputs:
- basis: float32 [4096, 64], P('shard')
- coeffs: float32 [14336, 64], P('shard')
The draws below stay inside these ranges and needn't reach their ends.
All inputs are finite; a program needn't handle non-finite values.
Results may differ from the reference program's by a relative error of at most 0.0033.
Values may be sent and summed in bfloat16 or wider, within the bound.
No kernel may reach another device: no remote copies, remote signals or barrier semaphores. Data moves between devices by JAX's collectives and lax.ppermute only.
A program may use at most 128 MiB of HBM per device.

```python
import math
import jax
import jax.numpy as jnp
from jax import lax

D = 4096
FF = 14336
R = 64
ITERS = 2
CLIENTS = 16


def draw_delta(key, part):
    first, second, third, fourth = jax.random.split(key, 4)
    base = jax.random.truncated_normal(first, -4.0, 4.0, (CLIENTS, D, FF), jnp.float32)
    top = math.log(10.0)
    slope = 2.0
    quiet_gain = 0.007
    row_scale = jnp.exp(top * jax.random.uniform(second, (CLIENTS, D, 1), jnp.float32))
    col_scale = jnp.exp(top * jax.random.uniform(third, (CLIENTS, 1, FF), jnp.float32))
    trend = jnp.sqrt(1.0 + slope * jnp.arange(D, dtype=jnp.float32) / D)[None, :, None]
    quiet_count = max(2, CLIENTS // 5)
    order = jax.random.permutation(fourth, CLIENTS)
    client_gain = jnp.where(order < quiet_count, jnp.float32(quiet_gain), jnp.float32(1.0))[:, None, None]
    return (base * row_scale * col_scale * trend * client_gain).astype(jnp.bfloat16)


def level_of(rng, extent, cuts, least, largest):
    loudness = 1.0
    for dim, parts in cuts:
        heights = jax.random.uniform(jax.random.fold_in(jax.random.fold_in(rng, 6), dim), (parts,), jnp.float32, least / len(cuts), largest / len(cuts))
        loudness = loudness * jnp.repeat(jnp.exp(heights), extent[dim] // parts).reshape((-1,) + (1,) * (len(extent) - 1 - dim))
    return loudness


def bell_draw(key, dims, width, reach, cuts=(), held_as=jnp.bfloat16):
    array = width * jax.random.normal(key, dims, jnp.float32)
    if cuts:
        array = array * level_of(key, dims, cuts, -0.22, 0.18)
    return jnp.clip(array, -reach, reach).astype(held_as)


def setup_inputs(seed: int = 0) -> dict:
    arg_keys = jax.random.split(jax.random.key(seed), 5)
    delta = draw_delta(jax.random.fold_in(arg_keys[4], 71), 0)
    start_coeffs = bell_draw(arg_keys[1], (FF, R), FF ** -0.5, 0.046875)
    noise_p = bell_draw(arg_keys[2], (ITERS, D, R), 1.0, 6.0, ((1, 8),), jnp.float32)
    noise_q = bell_draw(arg_keys[3], (ITERS, FF, R), 1.0, 6.0, ((1, 8),), jnp.float32)
    return dict(delta=delta, start_coeffs=start_coeffs, noise_p=noise_p, noise_q=noise_q)


EPS = 1e-06
CLIP_FRACTION = 0.5

def reference(delta, start_coeffs, noise_p, noise_q):

    def square_sum(carry, matrix):
        return (carry, jnp.sum(jnp.square(matrix.astype(jnp.float32))))
    _, sumsq = lax.scan(square_sum, jnp.float32(0.0), delta)
    scale = jnp.minimum(1.0, CLIP_FRACTION * math.sqrt(D * FF) / jnp.sqrt(sumsq + EPS))
    coeffs = start_coeffs.astype(jnp.float32)
    panel = jnp.zeros((D, R), jnp.float32)
    for step in range(ITERS):
        qb = coeffs.astype(jnp.bfloat16)
        level = jnp.sqrt(jnp.sum(jnp.square(coeffs)) / R)

        def add_panel(total, item):
            matrix, factor = item
            return (total + factor * jnp.dot(matrix.astype(jnp.float32), qb.astype(jnp.float32), preferred_element_type=jnp.float32), None)
        panel, _ = lax.scan(add_panel, jnp.zeros((D, R), jnp.float32), (delta, scale))
        panel = panel + level * noise_p[step]
        gram = jnp.dot(panel.T.astype(jnp.float32), panel.astype(jnp.float32), precision=lax.Precision.HIGHEST, preferred_element_type=jnp.float32)
        lower = jnp.linalg.cholesky(gram)
        panel = jax.scipy.linalg.solve_triangular(lower, panel.T, lower=True).T
        pb = panel.astype(jnp.bfloat16)

        def add_coeffs(total, item):
            matrix, factor = item
            return (total + factor * jnp.dot(matrix.T.astype(jnp.float32), pb.astype(jnp.float32), preferred_element_type=jnp.float32), None)
        coeffs, _ = lax.scan(add_coeffs, jnp.zeros((FF, R), jnp.float32), (delta, scale))
        coeffs = coeffs + noise_q[step]
    return (math.sqrt(D) * panel, coeffs)
```

```python
import functools
import math

import jax
import jax.numpy as jnp
from jax import lax
from jax.experimental import pallas as pl
from jax.experimental.pallas import tpu as pltpu
from jax.sharding import PartitionSpec as P

D = 4096
ITERS = 2
EPS = 1e-06
CLIP_FRACTION = 0.5

CLIENTS = 16
CHIPS_Y = 4
ROW_GROUP = 8


def client_pairs(flip_x, flip_z):
    return [(x * 4 + z, flip_x(x) * 4 + flip_z(z)) for x in range(4) for z in range(4)]


def keep(i):
    return i


def flip(i):
    return i ^ 1


def mirror(i):
    return 3 - i


CLIENT_STEPS = (
    client_pairs(keep, flip),
    client_pairs(keep, mirror),
    client_pairs(flip, keep),
    client_pairs(mirror, keep),
)
CORE_SWAP = [(i, i ^ 1) for i in range(8)]
SHARD_STEPS = (
    CORE_SWAP,
    [(y * 2 + c, flip(y) * 2 + c) for y in range(4) for c in range(2)],
    [(y * 2 + c, mirror(y) * 2 + c) for y in range(4) for c in range(2)],
)
SAME_CORE = [
    [k * 8 + 2 * y + c for y in range(CHIPS_Y) for k in range(CLIENTS)] for c in range(2)
]


def sum_steps(value, axis, steps):
    for pairs in steps:
        value = value + lax.ppermute(value, axis, pairs)
    return value


def first_panel_kernel(coeffs_ref, delta_ref, panel_ref, square_ref, level_ref, acc, squares, levels):
    step = pl.program_id(0)

    @pl.when(step == 0)
    def _():
        acc[...] = jnp.zeros_like(acc)
        squares[...] = jnp.zeros_like(squares)
        levels[...] = jnp.zeros_like(levels)

    coeffs = coeffs_ref[...]
    acc[...] += lax.dot_general(
        delta_ref[...], coeffs, (((1,), (1,)), ((), ())), preferred_element_type=jnp.float32
    )

    def rows(r, total):
        part = delta_ref[pl.ds(pl.multiple_of(r * 16, 16), 16), :].astype(jnp.float32)
        part = part * part
        return total + part.reshape(2, 8, part.shape[1]).sum(0)

    squares[...] = lax.fori_loop(0, delta_ref.shape[0] // 16, rows, squares[...])
    wide = coeffs.astype(jnp.float32)
    levels[...] += (wide * wide).reshape(-1, 8, wide.shape[1]).sum(0)

    @pl.when(step == pl.num_programs(0) - 1)
    def _():
        panel_ref[...] = acc[...].T
        square_ref[0, 0] = jnp.sum(squares[...])
        level_ref[0, 0] = jnp.sum(levels[...])


def first_panel(coeffs, mine, block=3584):
    rank = coeffs.shape[0]
    rows, columns = mine.shape
    scalar = jax.ShapeDtypeStruct((1, 1), jnp.float32)
    return pl.pallas_call(
        first_panel_kernel,
        grid=(columns // block,),
        in_specs=[
            pl.BlockSpec((rank, block), lambda i: (0, i)),
            pl.BlockSpec((rows, block), lambda i: (0, i)),
        ],
        out_specs=[
            pl.BlockSpec((rank, rows), lambda i: (0, 0)),
            pl.BlockSpec(memory_space=pltpu.SMEM),
            pl.BlockSpec(memory_space=pltpu.SMEM),
        ],
        out_shape=[jax.ShapeDtypeStruct((rank, rows), jnp.float32), scalar, scalar],
        scratch_shapes=[
            pltpu.VMEM((rows, rank), jnp.float32),
            pltpu.VMEM((8, block), jnp.float32),
            pltpu.VMEM((8, block), jnp.float32),
        ],
    )(coeffs, mine)


def panel_kernel(parity_ref, coeffs_ref, delta_ref, panel_ref, level_ref, acc, levels):
    step = pl.program_id(0)

    @pl.when(step == 0)
    def _():
        acc[...] = jnp.zeros_like(acc)
        levels[...] = jnp.zeros_like(levels)

    half = coeffs_ref.shape[-1]
    for h in range(2):
        coeffs = coeffs_ref[0, h]
        acc[...] += lax.dot_general(
            delta_ref[:, h * half : (h + 1) * half],
            coeffs,
            (((1,), (1,)), ((), ())),
            preferred_element_type=jnp.float32,
        )
        wide = coeffs.astype(jnp.float32)
        levels[...] += (wide * wide).reshape(-1, 8, half).sum(0)

    @pl.when(step == pl.num_programs(0) - 1)
    def _():
        panel_ref[...] = acc[...].T
        level_ref[0, 0] = jnp.sum(levels[...])


def panel_part(parity, coeffs, mine):
    steps, _, rank, half = coeffs.shape
    rows = mine.shape[0]
    return pl.pallas_call(
        panel_kernel,
        grid_spec=pltpu.PrefetchScalarGridSpec(
            num_scalar_prefetch=1,
            grid=(steps,),
            in_specs=[
                pl.BlockSpec((1, 2, rank, half), lambda i, parity: (i, 0, 0, 0)),
                pl.BlockSpec((rows, 2 * half), lambda i, parity: (0, 2 * i + parity[0])),
            ],
            out_specs=[
                pl.BlockSpec((rank, rows), lambda i, parity: (0, 0)),
                pl.BlockSpec(memory_space=pltpu.SMEM),
            ],
            scratch_shapes=[
                pltpu.VMEM((rows, rank), jnp.float32),
                pltpu.VMEM((8, half), jnp.float32),
            ],
        ),
        out_shape=[
            jax.ShapeDtypeStruct((rank, rows), jnp.float32),
            jax.ShapeDtypeStruct((1, 1), jnp.float32),
        ],
    )(parity, coeffs, mine)


def value_kernel(parity_ref, panel_ref, delta_ref, factor_ref, out_ref):
    value = factor_ref[0, 0] * lax.dot_general(
        panel_ref[...], delta_ref[...], (((1,), (0,)), ((), ())), preferred_element_type=jnp.float32
    )
    value = value.astype(out_ref.dtype)
    half = out_ref.shape[-1]
    out_ref[0, 0] = value[:, :half]
    out_ref[0, 1] = value[:, half:]


def value_part(parity, panel, mine, factor, dtype):
    rank, rows = panel.shape
    block = mine.shape[1] // (2 * CHIPS_Y)
    return pl.pallas_call(
        value_kernel,
        grid_spec=pltpu.PrefetchScalarGridSpec(
            num_scalar_prefetch=1,
            grid=(CHIPS_Y,),
            in_specs=[
                pl.BlockSpec((rank, rows), lambda i, parity: (0, 0)),
                pl.BlockSpec((rows, block), lambda i, parity: (0, 2 * i + parity[0])),
                pl.BlockSpec(memory_space=pltpu.SMEM),
            ],
            out_specs=pl.BlockSpec((1, 2, rank, block // 2), lambda i, parity: (i, 0, 0, 0)),
        ),
        out_shape=jax.ShapeDtypeStruct((CHIPS_Y, 2, rank, block // 2), dtype),
    )(parity, panel, mine, factor)


def orthonormal(panel):
    local_gram = lax.dot_general(
        panel,
        panel,
        (((1,), (1,)), ((), ())),
        precision=lax.Precision.HIGHEST,
        preferred_element_type=jnp.float32,
    )
    gram = sum_steps(local_gram, "shard", SHARD_STEPS)
    lower = jnp.linalg.cholesky(gram)
    return jax.scipy.linalg.solve_triangular(lower, panel, lower=True)


def on_device(delta, start_coeffs, noise_p, noise_q):
    mine = delta[0]
    coeffs = start_coeffs.T
    rank, columns = coeffs.shape
    panel_noise = noise_p.transpose(0, 2, 1)
    value_noise = noise_q.transpose(0, 2, 1)
    client = lax.axis_index("client")
    parity = lax.rem(lax.axis_index("shard"), 2).reshape(1)
    half = value_noise.shape[2] // 2
    group = rank // ROW_GROUP

    panel, squares, energy = first_panel(coeffs, mine)
    total = sum_steps(squares, "shard", SHARD_STEPS)
    count = D * columns
    factor = jnp.minimum(1.0, CLIP_FRACTION * math.sqrt(count) / jnp.sqrt(total + EPS))
    for step in range(ITERS):
        level = jnp.sqrt(energy / rank)
        panel = sum_steps(factor * panel, "client", CLIENT_STEPS) + level * panel_noise[step]
        panel = orthonormal(panel)
        rounded = panel.astype(jnp.bfloat16)
        away = value_part(1 - parity, rounded, mine, factor, jnp.bfloat16)
        away = lax.ppermute(away, "shard", CORE_SWAP)
        home = value_part(parity, rounded, mine, factor, jnp.float32)
        chip = (home + away.astype(jnp.float32)).astype(jnp.bfloat16)
        blocks = chip.reshape(CHIPS_Y * CLIENTS, ROW_GROUP, half)
        blocks = lax.all_to_all(
            blocks, ("client", "shard"), 0, 0, axis_index_groups=SAME_CORE
        )
        noise = lax.dynamic_slice(
            value_noise[step],
            (lax.rem(client, group) * ROW_GROUP, client // group * half),
            (ROW_GROUP, half),
        )
        value = jnp.sum(blocks.astype(jnp.float32), axis=0) + noise
        if step + 1 < ITERS:
            same = jnp.broadcast_to(value.astype(jnp.bfloat16), blocks.shape)
            same = lax.all_to_all(same, ("client", "shard"), 0, 0, axis_index_groups=SAME_CORE)
            same = same.reshape(CHIPS_Y, 2, rank, half)
            other = lax.ppermute(same, "shard", CORE_SWAP)
            panel, energy = panel_part(parity, same, mine)
            other_panel, other_energy = panel_part(1 - parity, other, mine)
            panel = panel + other_panel
            energy = energy + other_energy
        else:
            value = jnp.broadcast_to(value, (CLIENTS, ROW_GROUP, half))
            value = lax.all_to_all(value, "client", 0, 0)
            value = value.reshape(2, rank, half).transpose(1, 0, 2).reshape(rank, 2 * half)
    return (math.sqrt(D) * panel.T, value.T)


def solution(mesh):
    placed = (P("client", "shard", None), P(), P(None, "shard", None), P(None, "shard", None))
    return jax.shard_map(
        on_device,
        mesh=mesh,
        in_specs=placed,
        out_specs=(P("shard", None), P("shard", None)),
        check_vma=False,
    )
```

```python
import math

import jax
import jax.numpy as jnp
from jax import lax
from jax.experimental import pallas as pl
from jax.experimental.pallas import tpu as pltpu
from jax.sharding import PartitionSpec as P

D = 4096
ITERS = 2
EPS = 1e-06
CLIP_FRACTION = 0.5

CLIENTS = 16
CHIPS_Y = 4
ROW_GROUP = 8

IN_VMEM = pl.BlockSpec(memory_space=pltpu.VMEM)
IN_SMEM = pl.BlockSpec(memory_space=pltpu.SMEM)
SCALAR = jax.ShapeDtypeStruct((1, 1), jnp.float32)
KERNEL = pltpu.CompilerParams(vmem_limit_bytes=16 << 20)


def client_pairs(flip_x, flip_z):
    return [(x * 4 + z, flip_x(x) * 4 + flip_z(z)) for x in range(4) for z in range(4)]


def keep(i):
    return i


def flip(i):
    return i ^ 1


def mirror(i):
    return 3 - i


CLIENT_STEPS = (
    client_pairs(keep, flip),
    client_pairs(keep, mirror),
    client_pairs(flip, keep),
    client_pairs(mirror, keep),
)
CORE_SWAP = [(i, i ^ 1) for i in range(8)]
SHARD_STEPS = (
    CORE_SWAP,
    [(y * 2 + c, flip(y) * 2 + c) for y in range(4) for c in range(2)],
    [(y * 2 + c, mirror(y) * 2 + c) for y in range(4) for c in range(2)],
)
SAME_CORE = [
    [k * 8 + 2 * y + c for y in range(CHIPS_Y) for k in range(CLIENTS)] for c in range(2)
]


def sum_steps(value, axis, steps):
    for pairs in steps:
        value = value + lax.ppermute(value, axis, pairs)
    return value


def resident_kernel(delta_hbm, delta_ref, square_ref, sems):
    count = sems.shape[0]
    rows = delta_ref.shape[0] // count

    def copy(i):
        part = pl.ds(i * rows, rows)
        return pltpu.make_async_copy(delta_hbm.at[part, :], delta_ref.at[part, :], sems.at[i])

    for i in range(count):
        copy(i).start()
    total = jnp.zeros((8, 128), jnp.float32)
    for i in range(count):
        copy(i).wait()

        def column(c, total):
            part = delta_ref[pl.ds(i * rows, rows), pl.ds(pl.multiple_of(c * 512, 512), 512)]
            part = part.astype(jnp.float32)
            part = part * part
            part = part.reshape(rows // 8, 8, 512).sum(0)
            return total + (part[:, :128] + part[:, 128:256]) + (part[:, 256:384] + part[:, 384:])

        total = lax.fori_loop(0, delta_ref.shape[1] // 512, column, total)
    square_ref[0, 0] = jnp.sum(total)


def resident(mine, chunks=8):
    return pl.pallas_call(
        resident_kernel,
        in_specs=[pl.BlockSpec(memory_space=pl.ANY)],
        out_specs=[IN_VMEM, IN_SMEM],
        out_shape=[pltpu.VMEM(mine.shape, mine.dtype), SCALAR],
        scratch_shapes=[pltpu.SemaphoreType.DMA((chunks,))],
        compiler_params=KERNEL,
    )(mine)


def first_panel_kernel(coeffs_ref, delta_ref, panel_ref, level_ref):
    coeffs = coeffs_ref[...]
    panel_ref[...] = lax.dot_general(
        coeffs, delta_ref[...], (((1,), (1,)), ((), ())), preferred_element_type=jnp.float32
    )
    level_ref[0, 0] = energy_of(coeffs)


def energy_of(coeffs):
    wide = coeffs.astype(jnp.float32)
    return jnp.sum((wide * wide).reshape(-1, 8, wide.shape[-1]).sum(0))


def first_panel(coeffs, mine):
    return pl.pallas_call(
        first_panel_kernel,
        in_specs=[IN_VMEM, IN_VMEM],
        out_specs=[IN_VMEM, IN_SMEM],
        out_shape=[jax.ShapeDtypeStruct((coeffs.shape[0], mine.shape[0]), jnp.float32), SCALAR],
        compiler_params=KERNEL,
    )(coeffs, mine)


def shard_columns(parity, j, width):
    return pl.ds(pl.multiple_of((2 * j + parity) * width, width), width)


def panel_kernel(parity_ref, coeffs_ref, delta_ref, panel_ref, level_ref):
    parity = parity_ref[0]
    total = None
    energy = 0.0
    for j in range(CHIPS_Y):
        coeffs = jnp.concatenate([coeffs_ref[j, 0], coeffs_ref[j, 1]], axis=1)
        part = lax.dot_general(
            coeffs,
            delta_ref[:, shard_columns(parity, j, coeffs.shape[1])],
            (((1,), (1,)), ((), ())),
            preferred_element_type=jnp.float32,
        )
        total = part if total is None else total + part
        energy = energy + energy_of(coeffs)
    panel_ref[...] = total
    level_ref[0, 0] = energy


def panel_part(parity, coeffs, mine):
    return pl.pallas_call(
        panel_kernel,
        in_specs=[IN_SMEM, IN_VMEM, IN_VMEM],
        out_specs=[IN_VMEM, IN_SMEM],
        out_shape=[jax.ShapeDtypeStruct((coeffs.shape[2], mine.shape[0]), jnp.float32), SCALAR],
        compiler_params=KERNEL,
    )(parity, coeffs, mine)


def value_kernel(parity_ref, factor_ref, panel_ref, delta_ref, out_ref):
    parity = parity_ref[0]
    half = out_ref.shape[-1]
    for j in range(CHIPS_Y):
        value = factor_ref[0, 0] * lax.dot_general(
            panel_ref[...],
            delta_ref[:, shard_columns(parity, j, 2 * half)],
            (((1,), (0,)), ((), ())),
            preferred_element_type=jnp.float32,
        )
        value = value.astype(out_ref.dtype)
        out_ref[j, 0] = value[:, :half]
        out_ref[j, 1] = value[:, half:]


def value_part(parity, panel, mine, factor, dtype):
    half = mine.shape[1] // (4 * CHIPS_Y)
    return pl.pallas_call(
        value_kernel,
        in_specs=[IN_SMEM, IN_SMEM, IN_VMEM, IN_VMEM],
        out_specs=IN_VMEM,
        out_shape=jax.ShapeDtypeStruct((CHIPS_Y, 2, panel.shape[0], half), dtype),
        compiler_params=KERNEL,
    )(parity, factor, panel, mine)


def solve_kernel(gram_ref, panel_ref, out_ref, rounded_ref):
    rank = gram_ref.shape[0]
    lane = lax.broadcasted_iota(jnp.int32, (8, 2 * rank), 1)
    row = lax.broadcasted_iota(jnp.int32, (8, 2 * rank), 0)
    work = []
    for g in range(rank // 8):
        gram = jnp.concatenate([jnp.zeros((8, rank), jnp.float32), gram_ref[8 * g : 8 * g + 8, :]], axis=1)
        work.append(jnp.where(lane == row + 8 * g, 1.0, gram))
    for k in range(rank):
        g0, r0 = divmod(k, 8)
        columns = [
            jnp.broadcast_to(work[g][:, rank + k : rank + k + 1], (8, 2 * rank))
            for g in range(g0, rank // 8)
        ]
        pivot = jnp.broadcast_to(columns[0][r0 : r0 + 1, :], (8, 2 * rank))
        inverse = lax.rsqrt(pivot)
        inverse = inverse * (1.5 - 0.5 * pivot * inverse * inverse)
        scaled = jnp.broadcast_to(work[g0][r0 : r0 + 1, :], (8, 2 * rank)) * inverse
        for i, g in enumerate(range(g0, rank // 8)):
            lower = work[g] - (columns[i] * inverse) * scaled
            if g == g0:
                lower = jnp.where(row > r0, lower, jnp.where(row == r0, scaled, work[g]))
            work[g] = lower
    solve = jnp.concatenate([w[:, :rank] for w in work], axis=0)
    panel = lax.dot_general(
        solve,
        panel_ref[...],
        (((1,), (0,)), ((), ())),
        precision=lax.Precision.HIGHEST,
        preferred_element_type=jnp.float32,
    )
    out_ref[...] = panel
    rounded_ref[...] = panel.astype(rounded_ref.dtype)


def orthonormal(panel):
    local_gram = lax.dot_general(
        panel,
        panel,
        (((1,), (1,)), ((), ())),
        precision=lax.Precision.HIGHEST,
        preferred_element_type=jnp.float32,
    )
    gram = sum_steps(local_gram, "shard", SHARD_STEPS)
    return pl.pallas_call(
        solve_kernel,
        in_specs=[IN_VMEM, IN_VMEM],
        out_specs=[IN_VMEM, IN_VMEM],
        out_shape=[
            jax.ShapeDtypeStruct(panel.shape, jnp.float32),
            jax.ShapeDtypeStruct(panel.shape, jnp.bfloat16),
        ],
        compiler_params=KERNEL,
    )(gram, panel)


def on_device(delta, start_coeffs, noise_p, noise_q):
    mine = delta[0]
    coeffs = start_coeffs.T
    rank, columns = coeffs.shape
    panel_noise = noise_p.transpose(0, 2, 1)
    value_noise = noise_q.transpose(0, 2, 1)
    client = lax.axis_index("client")
    parity = lax.rem(lax.axis_index("shard"), 2).reshape(1)
    half = value_noise.shape[2] // 2
    group = rank // ROW_GROUP

    mine, squares = resident(mine)
    panel, energy = first_panel(coeffs, mine)
    total = sum_steps(squares, "shard", SHARD_STEPS)
    count = D * columns
    factor = jnp.minimum(1.0, CLIP_FRACTION * math.sqrt(count) / jnp.sqrt(total + EPS))
    for step in range(ITERS):
        level = jnp.sqrt(energy / rank)
        panel = sum_steps(factor * panel, "client", CLIENT_STEPS) + level * panel_noise[step]
        panel, rounded = orthonormal(panel)
        away = value_part(1 - parity, rounded, mine, factor, jnp.bfloat16)
        away = lax.ppermute(away, "shard", CORE_SWAP)
        home = value_part(parity, rounded, mine, factor, jnp.float32)
        chip = (home + away.astype(jnp.float32)).astype(jnp.bfloat16)
        blocks = chip.reshape(CHIPS_Y * CLIENTS, ROW_GROUP, half)
        blocks = lax.all_to_all(
            blocks, ("client", "shard"), 0, 0, axis_index_groups=SAME_CORE
        )
        noise = lax.dynamic_slice(
            value_noise[step],
            (lax.rem(client, group) * ROW_GROUP, client // group * half),
            (ROW_GROUP, half),
        )
        value = jnp.sum(blocks.astype(jnp.float32), axis=0) + noise
        if step + 1 < ITERS:
            same = jnp.broadcast_to(value.astype(jnp.bfloat16), blocks.shape)
            same = lax.all_to_all(same, ("client", "shard"), 0, 0, axis_index_groups=SAME_CORE)
            same = same.reshape(CHIPS_Y, 2, rank, half)
            other = lax.ppermute(same, "shard", CORE_SWAP)
            panel, energy = panel_part(parity, same, mine)
            other_panel, other_energy = panel_part(1 - parity, other, mine)
            panel = panel + other_panel
            energy = energy + other_energy
        else:
            value = jnp.broadcast_to(value, (CLIENTS, ROW_GROUP, half))
            value = lax.all_to_all(value, "client", 0, 0)
            value = value.reshape(2, rank, half).transpose(1, 0, 2).reshape(rank, 2 * half)
    return (math.sqrt(D) * panel.T, value.T)


def solution(mesh):
    placed = (P("client", "shard", None), P(), P(None, "shard", None), P(None, "shard", None))
    return jax.shard_map(
        on_device,
        mesh=mesh,
        in_specs=placed,
        out_specs=(P("shard", None), P("shard", None)),
        check_vma=False,
    )
```

```python
import functools
import math

import jax
import jax.numpy as jnp
from jax import lax
from jax.experimental import pallas as pl
from jax.experimental.pallas import tpu as pltpu
from jax.sharding import PartitionSpec as P

D = 4096
ITERS = 2
EPS = 1e-06
CLIP_FRACTION = 0.5

CLIENTS = 16
SHARDS = 8
CHIPS_Y = 4
ROW_GROUP = 8

IN_VMEM = pl.BlockSpec(memory_space=pltpu.VMEM)
IN_SMEM = pl.BlockSpec(memory_space=pltpu.SMEM)
SCALAR = jax.ShapeDtypeStruct((1, 1), jnp.float32)
KERNEL = pltpu.CompilerParams(vmem_limit_bytes=16 << 20)


def client_pairs(flip_x, flip_z):
    return [(x * 4 + z, flip_x(x) * 4 + flip_z(z)) for x in range(4) for z in range(4)]


def keep(i):
    return i


def flip(i):
    return i ^ 1


def mirror(i):
    return 3 - i


CLIENT_STEPS = (
    client_pairs(keep, flip),
    client_pairs(keep, mirror),
    client_pairs(flip, keep),
    client_pairs(mirror, keep),
)
CORE_SWAP = [(i, i ^ 1) for i in range(8)]
SAME_CORE = [
    [k * 8 + 2 * y + c for y in range(CHIPS_Y) for k in range(CLIENTS)] for c in range(2)
]


def energy_of(coeffs):
    wide = coeffs.astype(jnp.float32)
    return jnp.sum((wide * wide).reshape(-1, 8, wide.shape[-1]).sum(0))


def first_panel_kernel(coeffs_ref, delta_hbm, delta_ref, panel_ref, squares_ref, energy_ref, sems):
    count = sems.shape[0]
    width = delta_ref.shape[1] // count
    rows = delta_ref.shape[0]

    def copy(i):
        part = pl.ds(i * width, width)
        return pltpu.make_async_copy(delta_hbm.at[:, part], delta_ref.at[:, part], sems.at[i])

    for i in range(count):
        copy(i).start()
    squares = jnp.zeros((8, 128), jnp.float32)
    energy = 0.0
    panel = None
    for i in range(count):
        coeffs = coeffs_ref[:, i * width : (i + 1) * width]
        energy = energy + energy_of(coeffs)
        copy(i).wait()
        part = lax.dot_general(
            coeffs,
            delta_ref[:, i * width : (i + 1) * width],
            (((1,), (1,)), ((), ())),
            preferred_element_type=jnp.float32,
        )
        panel = part if panel is None else panel + part
        for c in range(width // 128):
            tile = delta_ref[:, i * width + c * 128 : i * width + (c + 1) * 128].astype(jnp.float32)
            squares = squares + (tile * tile).reshape(rows // 8, 8, 128).sum(0)
    panel_ref[...] = panel
    squares_ref[...] = jnp.broadcast_to(squares, squares_ref.shape)
    energy_ref[0, 0] = energy


def first_panel(coeffs, mine, chunks=7):
    return pl.pallas_call(
        first_panel_kernel,
        in_specs=[IN_VMEM, pl.BlockSpec(memory_space=pltpu.HBM)],
        out_specs=[IN_VMEM, IN_VMEM, IN_VMEM, IN_SMEM],
        out_shape=[
            pltpu.VMEM(mine.shape, mine.dtype),
            jax.ShapeDtypeStruct((coeffs.shape[0], mine.shape[0]), jnp.float32),
            jax.ShapeDtypeStruct((SHARDS, 8, 128), jnp.float32),
            SCALAR,
        ],
        scratch_shapes=[pltpu.SemaphoreType.DMA((chunks,))],
        compiler_params=KERNEL,
    )(coeffs, pltpu.with_memory_space_constraint(mine, pltpu.HBM))


def clip_kernel(squares_ref, panel_ref, out_ref, factor_ref, *, count):
    total = jnp.sum(squares_ref[...])
    bound = CLIP_FRACTION * math.sqrt(count)
    factor = jnp.minimum(1.0, bound / jnp.sqrt(jnp.full((8, 128), total + EPS, jnp.float32)))
    out_ref[...] = panel_ref[...] * factor[:1, :1]
    factor_ref[...] = factor


def clip(squares, panel, count):
    return pl.pallas_call(
        functools.partial(clip_kernel, count=count),
        in_specs=[IN_VMEM, IN_VMEM],
        out_specs=[IN_VMEM, IN_VMEM],
        out_shape=[
            jax.ShapeDtypeStruct(panel.shape, jnp.float32),
            jax.ShapeDtypeStruct((8, 128), jnp.float32),
        ],
        compiler_params=KERNEL,
    )(squares, panel)


def core_parity():
    return lax.rem(lax.axis_index("shard"), 2)


def shard_columns(parity, j, width):
    return pl.ds(pl.multiple_of((2 * j + parity) * width, width), width)


def panel_kernel(coeffs_ref, delta_ref, factor_ref, panel_ref, energy_ref, *, own):
    parity = core_parity() if own else 1 - core_parity()
    total = None
    energy = 0.0
    for j in range(CHIPS_Y):
        coeffs = jnp.concatenate([coeffs_ref[j, 0], coeffs_ref[j, 1]], axis=1)
        part = lax.dot_general(
            coeffs,
            delta_ref[:, shard_columns(parity, j, coeffs.shape[1])],
            (((1,), (1,)), ((), ())),
            preferred_element_type=jnp.float32,
        )
        total = part if total is None else total + part
        energy = energy + energy_of(coeffs)
    panel_ref[...] = total * factor_ref[:1, :1]
    energy_ref[0, 0] = energy


def panel_part(coeffs, mine, factor, own):
    return pl.pallas_call(
        functools.partial(panel_kernel, own=own),
        in_specs=[IN_VMEM, IN_VMEM, IN_VMEM],
        out_specs=[IN_VMEM, IN_SMEM],
        out_shape=[jax.ShapeDtypeStruct((coeffs.shape[2], mine.shape[0]), jnp.float32), SCALAR],
        compiler_params=KERNEL,
    )(coeffs, mine, factor)


def value_kernel(factor_ref, panel_ref, delta_ref, out_ref, *, own):
    parity = core_parity() if own else 1 - core_parity()
    half = out_ref.shape[-1]
    for j in range(CHIPS_Y):
        value = factor_ref[:1, :1] * lax.dot_general(
            panel_ref[...],
            delta_ref[:, shard_columns(parity, j, 2 * half)],
            (((1,), (0,)), ((), ())),
            preferred_element_type=jnp.float32,
        )
        value = value.astype(out_ref.dtype)
        out_ref[j, 0] = value[:, :half]
        out_ref[j, 1] = value[:, half:]


def value_part(panel, mine, factor, own, dtype):
    half = mine.shape[1] // (4 * CHIPS_Y)
    return pl.pallas_call(
        functools.partial(value_kernel, own=own),
        in_specs=[IN_VMEM, IN_VMEM, IN_VMEM],
        out_specs=IN_VMEM,
        out_shape=jax.ShapeDtypeStruct((CHIPS_Y, 2, panel.shape[0], half), dtype),
        compiler_params=KERNEL,
    )(factor, panel, mine)


def merge_kernel(blocks_ref, noise_ref, out_ref, *, step):
    client = lax.axis_index("client")
    total = jnp.zeros(blocks_ref.shape[1:], jnp.float32)
    for i in range(blocks_ref.shape[0]):
        total = total + blocks_ref[i].astype(jnp.float32)
    rows, half = total.shape
    group = noise_ref.shape[1] // rows
    row = pl.ds(pl.multiple_of(lax.rem(client, group) * rows, rows), rows)
    lane = pl.ds(pl.multiple_of(lax.div(client, group) * half, half), half)
    total = total + noise_ref[step, row, lane]
    out_ref[...] = jnp.broadcast_to(total.astype(out_ref.dtype), out_ref.shape)


def merge(blocks, noise, step, copies, dtype):
    return pl.pallas_call(
        functools.partial(merge_kernel, step=step),
        in_specs=[IN_VMEM, IN_VMEM],
        out_specs=IN_VMEM,
        out_shape=jax.ShapeDtypeStruct((copies,) + blocks.shape[1:], dtype),
        compiler_params=KERNEL,
    )(blocks, noise)


def gram_kernel(energy_ref, here_ref, there_ref, noise_ref, panel_ref, gram_ref, *, step):
    rank = here_ref.shape[0]
    level = jnp.sqrt(jnp.full((8, 128), energy_ref[0, 0] / rank, jnp.float32))[:1, :1]
    panel = (here_ref[...] + there_ref[...]) + level * noise_ref[step]
    panel_ref[...] = panel
    gram = lax.dot_general(
        panel,
        panel,
        (((1,), (1,)), ((), ())),
        precision=lax.Precision.HIGHEST,
        preferred_element_type=jnp.float32,
    )
    gram = jnp.concatenate([gram[: rank // 2], gram[rank // 2 :]], axis=1)
    gram_ref[...] = jnp.broadcast_to(gram, gram_ref.shape)


def noisy_gram(energy, here, there, noise, step):
    rank = here.shape[0]
    return pl.pallas_call(
        functools.partial(gram_kernel, step=step),
        in_specs=[IN_SMEM, IN_VMEM, IN_VMEM, IN_VMEM],
        out_specs=[IN_VMEM, IN_VMEM],
        out_shape=[
            jax.ShapeDtypeStruct(here.shape, jnp.float32),
            jax.ShapeDtypeStruct((SHARDS, rank // 2, 2 * rank), jnp.float32),
        ],
        compiler_params=KERNEL,
    )(energy, here, there, noise)


def inverse_factor(gram):
    rank = gram.shape[0]
    groups = rank // 8
    lane = lax.broadcasted_iota(jnp.int32, (8, 2 * rank), 1)
    row = lax.broadcasted_iota(jnp.int32, (8, 2 * rank), 0)

    def spread(tile, r):
        return jnp.broadcast_to(tile[r : r + 1, :], tile.shape)

    work = []
    for g in range(groups):
        right = jnp.concatenate(
            [jnp.zeros((8, rank), jnp.float32), gram[8 * g : 8 * g + 8, :]], axis=1
        )
        work.append(jnp.where(lane == row + 8 * g, 1.0, right))
    for b in range(groups):
        column = [
            [
                jnp.broadcast_to(
                    work[g][:, rank + 8 * b + j : rank + 8 * b + j + 1], (8, 2 * rank)
                )
                for g in range(b, groups)
            ]
            for j in range(8)
        ]
        diagonal = jnp.zeros((8, 2 * rank), jnp.float32)
        for j in range(8):
            pivot = spread(column[j][0], j)
            diagonal = jnp.where(row == j, pivot, diagonal)
            inverse = 1.0 / pivot
            ratio = [c * inverse for c in column[j]]
            ratio[0] = jnp.where(row > j, ratio[0], 0.0)
            for k in range(j + 1, 8):
                top = spread(column[k][0], j)
                column[k] = [c - f * top for c, f in zip(column[k], ratio)]
            top = spread(work[b], j)
            for g in range(b, groups):
                work[g] = work[g] - ratio[g - b] * top
        work[b] = work[b] * (1.0 / jnp.sqrt(diagonal))
    return jnp.concatenate([w[:, :rank] for w in work], axis=0)


def solve_kernel(gram_ref, panel_ref, rounded_ref, *basis_ref):
    gram = gram_ref[0]
    for i in range(1, gram_ref.shape[0]):
        gram = gram + gram_ref[i]
    rank = panel_ref.shape[0]
    gram = jnp.concatenate([gram[:, :rank], gram[:, rank:]], axis=0)
    panel = lax.dot_general(
        inverse_factor(gram),
        panel_ref[...],
        (((1,), (0,)), ((), ())),
        precision=lax.Precision.HIGHEST,
        preferred_element_type=jnp.float32,
    )
    rounded_ref[...] = panel.astype(rounded_ref.dtype)
    for ref in basis_ref:
        ref[...] = math.sqrt(D) * panel


def orthonormal(grams, panel, last):
    shapes = [jax.ShapeDtypeStruct(panel.shape, jnp.bfloat16)]
    if last:
        shapes.append(jax.ShapeDtypeStruct(panel.shape, jnp.float32))
    return pl.pallas_call(
        solve_kernel,
        in_specs=[IN_VMEM, IN_VMEM],
        out_specs=[IN_VMEM] * len(shapes),
        out_shape=shapes,
        compiler_params=KERNEL,
    )(grams, panel)


def on_device(delta, start_coeffs, noise_p, noise_q):
    coeffs = start_coeffs.T
    rank, columns = coeffs.shape
    panel_noise = noise_p.transpose(0, 2, 1)
    value_noise = noise_q.transpose(0, 2, 1)

    mine, panel, squares, energy = first_panel(coeffs, delta[0])
    squares = lax.all_to_all(squares, "shard", 0, 0)
    panel, factor = clip(squares, panel, D * columns)
    for step in range(ITERS):
        last = step + 1 == ITERS
        for pairs in CLIENT_STEPS[:-1]:
            panel = panel + lax.ppermute(panel, "client", pairs)
        there = lax.ppermute(panel, "client", CLIENT_STEPS[-1])
        panel, grams = noisy_gram(energy, panel, there, panel_noise, step)
        grams = lax.all_to_all(grams, "shard", 0, 0)
        rounded, *basis = orthonormal(grams, panel, last)
        away = value_part(rounded, mine, factor, False, jnp.bfloat16)
        away = lax.ppermute(away, "shard", CORE_SWAP)
        home = value_part(rounded, mine, factor, True, jnp.float32)
        chip = (home + away.astype(jnp.float32)).astype(jnp.bfloat16)
        blocks = chip.reshape(CHIPS_Y * CLIENTS, ROW_GROUP, chip.shape[-1])
        blocks = lax.all_to_all(
            blocks, ("client", "shard"), 0, 0, axis_index_groups=SAME_CORE
        )
        if last:
            value = merge(blocks, value_noise, step, CLIENTS, jnp.float32)
            value = lax.all_to_all(value, "client", 0, 0)
        else:
            same = merge(blocks, value_noise, step, CHIPS_Y * CLIENTS, jnp.bfloat16)
            same = lax.all_to_all(same, ("client", "shard"), 0, 0, axis_index_groups=SAME_CORE)
            same = same.reshape(chip.shape)
            other = lax.ppermute(same, "shard", CORE_SWAP)
            panel, energy = panel_part(same, mine, factor, True)
            other_panel, other_energy = panel_part(other, mine, factor, False)
            panel = panel + other_panel
            energy = energy + other_energy
    half = value.shape[-1]
    value = value.reshape(2, rank, half).transpose(1, 0, 2).reshape(rank, 2 * half)
    return (basis[0].T, value.T)


def solution(mesh):
    placed = (P("client", "shard", None), P(), P(None, "shard", None), P(None, "shard", None))
    return jax.shard_map(
        on_device,
        mesh=mesh,
        in_specs=placed,
        out_specs=(P("shard", None), P("shard", None)),
        check_vma=False,
    )
```

```python
import functools
import math

import jax
import jax.numpy as jnp
from jax import lax
from jax.experimental import pallas as pl
from jax.experimental.pallas import tpu as pltpu
from jax.sharding import PartitionSpec as P

D = 4096
ITERS = 2
EPS = 1e-06
CLIP_FRACTION = 0.5

CLIENTS = 16
SHARDS = 8
CHIPS_Y = 4
ROW_GROUP = 8
FIRST_PARTS = 2

IN_VMEM = pl.BlockSpec(memory_space=pltpu.VMEM)
IN_SMEM = pl.BlockSpec(memory_space=pltpu.SMEM)
SCALAR = jax.ShapeDtypeStruct((1, 1), jnp.float32)
KERNEL = pltpu.CompilerParams(vmem_limit_bytes=16 << 20)


def client_pairs(flip_x, flip_z):
    return [(x * 4 + z, flip_x(x) * 4 + flip_z(z)) for x in range(4) for z in range(4)]


def keep(i):
    return i


def flip(i):
    return i ^ 1


def mirror(i):
    return 3 - i


ALONG_Z = (client_pairs(keep, flip), client_pairs(keep, mirror))
ALONG_X = (client_pairs(flip, keep), client_pairs(mirror, keep))
CLIENT_STEPS = tuple(zip(ALONG_Z + ALONG_X, ALONG_X + ALONG_Z))
CORE_SWAP = [(i, i ^ 1) for i in range(8)]
SHARD_STEPS = (
    CORE_SWAP,
    [(y * 2 + c, flip(y) * 2 + c) for y in range(4) for c in range(2)],
    [(y * 2 + c, mirror(y) * 2 + c) for y in range(4) for c in range(2)],
)
SAME_CORE = [
    [k * 8 + 2 * y + c for y in range(CHIPS_Y) for k in range(CLIENTS)] for c in range(2)
]


def energy_of(coeffs):
    wide = coeffs.astype(jnp.float32)
    return jnp.sum((wide * wide).reshape(-1, 8, wide.shape[-1]).sum(0))


def resident_kernel(delta_hbm, delta_ref, squares_ref, sems):
    count = sems.shape[0]
    rows = delta_ref.shape[0] // count

    def copy(i):
        part = pl.ds(i * rows, rows)
        return pltpu.make_async_copy(delta_hbm.at[part, :], delta_ref.at[part, :], sems.at[i])

    for i in range(count):
        copy(i).start()
    total = jnp.zeros((8, 128), jnp.float32)
    for i in range(count):
        copy(i).wait()

        def column(c, total):
            part = delta_ref[pl.ds(i * rows, rows), pl.ds(pl.multiple_of(c * 512, 512), 512)]
            part = part.astype(jnp.float32)
            part = part * part
            part = part.reshape(rows // 8, 8, 512).sum(0)
            return total + (part[:, :128] + part[:, 128:256]) + (part[:, 256:384] + part[:, 384:])

        total = lax.fori_loop(0, delta_ref.shape[1] // 512, column, total)
    squares_ref[...] = total


def resident(mine, chunks=8):
    return pl.pallas_call(
        resident_kernel,
        in_specs=[pl.BlockSpec(memory_space=pltpu.HBM)],
        out_specs=[IN_VMEM, IN_VMEM],
        out_shape=[
            pltpu.VMEM(mine.shape, mine.dtype),
            jax.ShapeDtypeStruct((8, 128), jnp.float32),
        ],
        scratch_shapes=[pltpu.SemaphoreType.DMA((chunks,))],
        compiler_params=KERNEL,
    )(pltpu.with_memory_space_constraint(mine, pltpu.HBM))


def first_panel_kernel(coeffs_ref, delta_ref, panel_ref, energy_ref, *, part):
    width = coeffs_ref.shape[1] // FIRST_PARTS
    coeffs = coeffs_ref[:, part * width : (part + 1) * width]
    panel_ref[...] = lax.dot_general(
        coeffs,
        delta_ref[:, part * width : (part + 1) * width],
        (((1,), (1,)), ((), ())),
        preferred_element_type=jnp.float32,
    )
    energy_ref[0, 0] = energy_of(coeffs)


def first_panel(coeffs, mine, part):
    return pl.pallas_call(
        functools.partial(first_panel_kernel, part=part),
        in_specs=[IN_VMEM, IN_VMEM],
        out_specs=[IN_VMEM, IN_SMEM],
        out_shape=[jax.ShapeDtypeStruct((coeffs.shape[0], mine.shape[0]), jnp.float32), SCALAR],
        compiler_params=KERNEL,
    )(coeffs, mine)


def clip_kernel(here_ref, there_ref, *refs, count):
    *parts, low_ref, high_ref, factor_ref = refs
    total = jnp.sum(here_ref[...] + there_ref[...])
    bound = CLIP_FRACTION * math.sqrt(count)
    factor = jnp.minimum(1.0, bound / jnp.sqrt(jnp.full((8, 128), total + EPS, jnp.float32)))
    panel = parts[0][...]
    for part in parts[1:]:
        panel = panel + part[...]
    panel = panel * factor[:1, :1]
    half = low_ref.shape[0]
    low_ref[...] = panel[:half]
    high_ref[...] = panel[half:]
    factor_ref[...] = factor


def clip(here, there, parts, count):
    rank, rows = parts[0].shape
    half = jax.ShapeDtypeStruct((rank // 2, rows), jnp.float32)
    return pl.pallas_call(
        functools.partial(clip_kernel, count=count),
        in_specs=[IN_VMEM] * (2 + len(parts)),
        out_specs=[IN_VMEM] * 3,
        out_shape=[half, half, jax.ShapeDtypeStruct((8, 128), jnp.float32)],
        compiler_params=KERNEL,
    )(here, there, *parts)


def core_parity():
    return lax.rem(lax.axis_index("shard"), 2)


def shard_columns(parity, j, width):
    return pl.ds(pl.multiple_of((2 * j + parity) * width, width), width)


def panel_of(parity, coeffs_ref, delta_ref):
    total = None
    energy = 0.0
    for j in range(CHIPS_Y):
        coeffs = jnp.concatenate([coeffs_ref[j, 0], coeffs_ref[j, 1]], axis=1)
        part = lax.dot_general(
            coeffs,
            delta_ref[:, shard_columns(parity, j, coeffs.shape[1])],
            (((1,), (1,)), ((), ())),
            preferred_element_type=jnp.float32,
        )
        total = part if total is None else total + part
        energy = energy + energy_of(coeffs)
    return total, energy


def own_panel_kernel(coeffs_ref, delta_ref, panel_ref, energy_ref):
    panel_ref[...], energy_ref[0, 0] = panel_of(core_parity(), coeffs_ref, delta_ref)


def own_panel(coeffs, mine):
    return pl.pallas_call(
        own_panel_kernel,
        in_specs=[IN_VMEM, IN_VMEM],
        out_specs=[IN_VMEM, IN_SMEM],
        out_shape=[jax.ShapeDtypeStruct((coeffs.shape[2], mine.shape[0]), jnp.float32), SCALAR],
        compiler_params=KERNEL,
    )(coeffs, mine)


def whole_panel_kernel(coeffs_ref, delta_ref, factor_ref, own_ref, low_ref, high_ref, energy_ref):
    panel, energy = panel_of(1 - core_parity(), coeffs_ref, delta_ref)
    panel = (panel + own_ref[...]) * factor_ref[:1, :1]
    half = low_ref.shape[0]
    low_ref[...] = panel[:half]
    high_ref[...] = panel[half:]
    energy_ref[0, 0] = energy


def whole_panel(coeffs, mine, factor, own):
    half = jax.ShapeDtypeStruct((own.shape[0] // 2, own.shape[1]), jnp.float32)
    return pl.pallas_call(
        whole_panel_kernel,
        in_specs=[IN_VMEM] * 4,
        out_specs=[IN_VMEM, IN_VMEM, IN_SMEM],
        out_shape=[half, half, SCALAR],
        compiler_params=KERNEL,
    )(coeffs, mine, factor, own)


def value_kernel(factor_ref, panel_ref, delta_ref, out_ref, *, own):
    parity = core_parity() if own else 1 - core_parity()
    half = out_ref.shape[-1]
    for j in range(CHIPS_Y):
        value = factor_ref[:1, :1] * lax.dot_general(
            panel_ref[...],
            delta_ref[:, shard_columns(parity, j, 2 * half)],
            (((1,), (0,)), ((), ())),
            preferred_element_type=jnp.float32,
        )
        value = value.astype(out_ref.dtype)
        out_ref[j, 0] = value[:, :half]
        out_ref[j, 1] = value[:, half:]


def value_part(panel, mine, factor, own, dtype):
    half = mine.shape[1] // (4 * CHIPS_Y)
    return pl.pallas_call(
        functools.partial(value_kernel, own=own),
        in_specs=[IN_VMEM, IN_VMEM, IN_VMEM],
        out_specs=IN_VMEM,
        out_shape=jax.ShapeDtypeStruct((CHIPS_Y, 2, panel.shape[0], half), dtype),
        compiler_params=KERNEL,
    )(factor, panel, mine)


def merge_kernel(blocks_ref, noise_ref, out_ref, *, step):
    client = lax.axis_index("client")
    total = jnp.zeros(blocks_ref.shape[1:], jnp.float32)
    for i in range(blocks_ref.shape[0]):
        total = total + blocks_ref[i].astype(jnp.float32)
    rows, half = total.shape
    group = noise_ref.shape[1] // rows
    row = pl.ds(pl.multiple_of(lax.rem(client, group) * rows, rows), rows)
    lane = pl.ds(pl.multiple_of(lax.div(client, group) * half, half), half)
    total = total + noise_ref[step, row, lane]
    out_ref[...] = jnp.broadcast_to(total.astype(out_ref.dtype), out_ref.shape)


def merge(blocks, noise, step, copies, dtype):
    return pl.pallas_call(
        functools.partial(merge_kernel, step=step),
        in_specs=[IN_VMEM, IN_VMEM],
        out_specs=IN_VMEM,
        out_shape=jax.ShapeDtypeStruct((copies,) + blocks.shape[1:], dtype),
        compiler_params=KERNEL,
    )(blocks, noise)


def gram_kernel(*refs, step, energies):
    parts, (low_ref, low_there, high_ref, high_there, noise_ref, panel_ref, gram_ref) = (
        refs[:energies],
        refs[energies:],
    )
    energy = parts[0][0, 0]
    for part in parts[1:]:
        energy = energy + part[0, 0]
    rank = panel_ref.shape[0]
    level = jnp.sqrt(jnp.full((8, 128), energy / rank, jnp.float32))[:1, :1]
    low = low_ref[...] + low_there[...]
    high = high_ref[...] + high_there[...]
    panel = jnp.concatenate([low, high], axis=0) + level * noise_ref[step]
    panel_ref[...] = panel
    gram = lax.dot_general(
        panel,
        panel,
        (((1,), (1,)), ((), ())),
        precision=lax.Precision.HIGHEST,
        preferred_element_type=jnp.float32,
    )
    gram = jnp.concatenate([gram[: rank // 2], gram[rank // 2 :]], axis=1)
    gram_ref[...] = jnp.broadcast_to(gram, gram_ref.shape)


def noisy_gram(energies, halves, noise, step):
    rank, rows = noise.shape[1:]
    return pl.pallas_call(
        functools.partial(gram_kernel, step=step, energies=len(energies)),
        in_specs=[IN_SMEM] * len(energies) + [IN_VMEM] * 5,
        out_specs=[IN_VMEM, IN_VMEM],
        out_shape=[
            jax.ShapeDtypeStruct((rank, rows), jnp.float32),
            jax.ShapeDtypeStruct((SHARDS, rank // 2, 2 * rank), jnp.float32),
        ],
        compiler_params=KERNEL,
    )(*energies, *halves, noise)


def inverse_factor(gram):
    rank = gram.shape[0]
    groups = rank // 8
    lane = lax.broadcasted_iota(jnp.int32, (8, 2 * rank), 1)
    row = lax.broadcasted_iota(jnp.int32, (8, 2 * rank), 0)

    def spread(tile, r):
        return jnp.broadcast_to(tile[r : r + 1, :], tile.shape)

    work = []
    for g in range(groups):
        right = jnp.concatenate(
            [jnp.zeros((8, rank), jnp.float32), gram[8 * g : 8 * g + 8, :]], axis=1
        )
        work.append(jnp.where(lane == row + 8 * g, 1.0, right))
    for b in range(groups):
        column = [
            [
                jnp.broadcast_to(
                    work[g][:, rank + 8 * b + j : rank + 8 * b + j + 1], (8, 2 * rank)
                )
                for g in range(b, groups)
            ]
            for j in range(8)
        ]
        diagonal = jnp.zeros((8, 2 * rank), jnp.float32)
        for j in range(8):
            pivot = spread(column[j][0], j)
            diagonal = jnp.where(row == j, pivot, diagonal)
            inverse = 1.0 / pivot
            ratio = [c * inverse for c in column[j]]
            ratio[0] = jnp.where(row > j, ratio[0], 0.0)
            for k in range(j + 1, 8):
                top = spread(column[k][0], j)
                column[k] = [c - f * top for c, f in zip(column[k], ratio)]
            top = spread(work[b], j)
            for g in range(b, groups):
                work[g] = work[g] - ratio[g - b] * top
        work[b] = work[b] * (1.0 / jnp.sqrt(diagonal))
    return jnp.concatenate([w[:, :rank] for w in work], axis=0)


def solve_kernel(gram_ref, panel_ref, rounded_ref, *basis_ref):
    gram = gram_ref[0]
    for i in range(1, gram_ref.shape[0]):
        gram = gram + gram_ref[i]
    rank = panel_ref.shape[0]
    gram = jnp.concatenate([gram[:, :rank], gram[:, rank:]], axis=0)
    panel = lax.dot_general(
        inverse_factor(gram),
        panel_ref[...],
        (((1,), (0,)), ((), ())),
        precision=lax.Precision.HIGHEST,
        preferred_element_type=jnp.float32,
    )
    rounded_ref[...] = panel.astype(rounded_ref.dtype)
    for ref in basis_ref:
        ref[...] = math.sqrt(D) * panel


def orthonormal(grams, panel, last):
    shapes = [jax.ShapeDtypeStruct(panel.shape, jnp.bfloat16)]
    if last:
        shapes.append(jax.ShapeDtypeStruct(panel.shape, jnp.float32))
    return pl.pallas_call(
        solve_kernel,
        in_specs=[IN_VMEM, IN_VMEM],
        out_specs=[IN_VMEM] * len(shapes),
        out_shape=shapes,
        compiler_params=KERNEL,
    )(grams, panel)


def on_device(delta, start_coeffs, noise_p, noise_q):
    coeffs = start_coeffs.T
    rank, columns = coeffs.shape
    panel_noise = noise_p.transpose(0, 2, 1)
    value_noise = noise_q.transpose(0, 2, 1)

    mine, squares = resident(delta[0])
    first, first_energy = first_panel(coeffs, mine, 0)
    second, second_energy = first_panel(coeffs, mine, 1)
    squares = squares + lax.ppermute(squares, "shard", SHARD_STEPS[0])
    squares = squares + lax.ppermute(squares, "shard", SHARD_STEPS[1])
    squares, first = lax.optimization_barrier((squares, first))
    parts = (first, second)
    energies = (first_energy, second_energy)
    there = lax.ppermute(squares, "shard", SHARD_STEPS[-1])
    low, high, factor = clip(squares, there, parts, D * columns)
    for step in range(ITERS):
        last = step + 1 == ITERS
        for low_pairs, high_pairs in CLIENT_STEPS[:-1]:
            low_there = lax.ppermute(low, "client", low_pairs)
            high_there = lax.ppermute(high, "client", high_pairs)
            low = low + low_there
            high = high + high_there
        low_pairs, high_pairs = CLIENT_STEPS[-1]
        low_there = lax.ppermute(low, "client", low_pairs)
        high_there = lax.ppermute(high, "client", high_pairs)
        halves = (low, low_there, high, high_there)
        panel, grams = noisy_gram(energies, halves, panel_noise, step)
        grams = lax.all_to_all(grams, "shard", 0, 0)
        rounded, *basis = orthonormal(grams, panel, last)
        away = value_part(rounded, mine, factor, False, jnp.bfloat16)
        away = lax.ppermute(away, "shard", CORE_SWAP)
        home = value_part(rounded, mine, factor, True, jnp.float32)
        chip = (home + away.astype(jnp.float32)).astype(jnp.bfloat16)
        blocks = chip.reshape(CHIPS_Y * CLIENTS, ROW_GROUP, chip.shape[-1])
        blocks = lax.all_to_all(
            blocks, ("client", "shard"), 0, 0, axis_index_groups=SAME_CORE
        )
        if last:
            value = merge(blocks, value_noise, step, CLIENTS, jnp.float32)
            value = lax.all_to_all(value, "client", 0, 0)
        else:
            same = merge(blocks, value_noise, step, CHIPS_Y * CLIENTS, jnp.bfloat16)
            same = lax.all_to_all(same, ("client", "shard"), 0, 0, axis_index_groups=SAME_CORE)
            same = same.reshape(chip.shape)
            other = lax.ppermute(same, "shard", CORE_SWAP)
            own, own_energy = own_panel(same, mine)
            low, high, other_energy = whole_panel(other, mine, factor, own)
            energies = (own_energy, other_energy)
    half = value.shape[-1]
    value = value.reshape(2, rank, half).transpose(1, 0, 2).reshape(rank, 2 * half)
    return (basis[0].T, value.T)


def solution(mesh):
    placed = (P("client", "shard", None), P(), P(None, "shard", None), P(None, "shard", None))
    return jax.shard_map(
        on_device,
        mesh=mesh,
        in_specs=placed,
        out_specs=(P("shard", None), P("shard", None)),
        check_vma=False,
    )
```

```python
import functools
import math

import jax
import jax.numpy as jnp
from jax import lax
from jax.experimental import pallas as pl
from jax.experimental.pallas import tpu as pltpu
from jax.sharding import PartitionSpec as P

D = 4096
ITERS = 2
EPS = 1e-06
CLIP_FRACTION = 0.5

CLIENTS = 16
SHARDS = 8
CHIPS_Y = 4
ROW_GROUP = 8
FIRST_PARTS = 2

IN_VMEM = pl.BlockSpec(memory_space=pltpu.VMEM)
IN_SMEM = pl.BlockSpec(memory_space=pltpu.SMEM)
SCALAR = jax.ShapeDtypeStruct((1, 1), jnp.float32)
KERNEL = pltpu.CompilerParams(vmem_limit_bytes=16 << 20)


def client_pairs(flip_x, flip_z):
    return [(x * 4 + z, flip_x(x) * 4 + flip_z(z)) for x in range(4) for z in range(4)]


def keep(i):
    return i


def flip(i):
    return i ^ 1


def mirror(i):
    return 3 - i


ALONG_Z = (client_pairs(keep, flip), client_pairs(keep, mirror))
ALONG_X = (client_pairs(flip, keep), client_pairs(mirror, keep))
CLIENT_STEPS = tuple(zip(ALONG_Z + ALONG_X, ALONG_X + ALONG_Z))
CORE_SWAP = [(i, i ^ 1) for i in range(8)]
SHARD_STEPS = (
    CORE_SWAP,
    [(y * 2 + c, flip(y) * 2 + c) for y in range(4) for c in range(2)],
    [(y * 2 + c, mirror(y) * 2 + c) for y in range(4) for c in range(2)],
)
SAME_CORE = [
    [
        (g * 2 + h) * SHARDS + 2 * y + c
        for y in range(CHIPS_Y)
        for h in range(2)
        for g in range(CLIENTS // 2)
    ]
    for c in range(2)
]


def energy_of(coeffs):
    wide = coeffs.astype(jnp.float32)
    return jnp.sum((wide * wide).reshape(-1, 8, wide.shape[-1]).sum(0))


def resident_kernel(delta_hbm, delta_ref, squares_ref, sems):
    count = sems.shape[0]
    rows = delta_ref.shape[0] // count

    def copy(i):
        part = pl.ds(i * rows, rows)
        return pltpu.make_async_copy(delta_hbm.at[part, :], delta_ref.at[part, :], sems.at[i])

    for i in range(count):
        copy(i).start()
    total = jnp.zeros((8, 128), jnp.float32)
    for i in range(count):
        copy(i).wait()

        def column(c, total):
            part = delta_ref[pl.ds(i * rows, rows), pl.ds(pl.multiple_of(c * 1024, 1024), 1024)]
            part = part.astype(jnp.float32)
            return total + (part * part).reshape(rows // 8, 8, 1024).sum(0)

        wide = lax.fori_loop(
            0, delta_ref.shape[1] // 1024, column, jnp.zeros((8, 1024), jnp.float32), unroll=2
        )
        for k in range(8):
            total = total + wide[:, k * 128 : (k + 1) * 128]
    squares_ref[...] = total


def resident(mine, chunks=16):
    return pl.pallas_call(
        resident_kernel,
        in_specs=[pl.BlockSpec(memory_space=pltpu.HBM)],
        out_specs=[IN_VMEM, IN_VMEM],
        out_shape=[
            pltpu.VMEM(mine.shape, mine.dtype),
            jax.ShapeDtypeStruct((8, 128), jnp.float32),
        ],
        scratch_shapes=[pltpu.SemaphoreType.DMA((chunks,))],
        compiler_params=KERNEL,
    )(pltpu.with_memory_space_constraint(mine, pltpu.HBM))


def first_panel_kernel(coeffs_ref, delta_ref, panel_ref, energy_ref, *, part):
    width = coeffs_ref.shape[1] // FIRST_PARTS
    coeffs = coeffs_ref[:, part * width : (part + 1) * width]
    panel_ref[...] = lax.dot_general(
        coeffs,
        delta_ref[:, part * width : (part + 1) * width],
        (((1,), (1,)), ((), ())),
        preferred_element_type=jnp.float32,
    )
    energy_ref[0, 0] = energy_of(coeffs)


def first_panel(coeffs, mine, part):
    return pl.pallas_call(
        functools.partial(first_panel_kernel, part=part),
        in_specs=[IN_VMEM, IN_VMEM],
        out_specs=[IN_VMEM, IN_SMEM],
        out_shape=[jax.ShapeDtypeStruct((coeffs.shape[0], mine.shape[0]), jnp.float32), SCALAR],
        compiler_params=KERNEL,
    )(coeffs, mine)


def clip_kernel(here_ref, there_ref, *refs, count):
    *parts, low_ref, high_ref, factor_ref = refs
    total = jnp.sum(here_ref[...] + there_ref[...])
    bound = CLIP_FRACTION * math.sqrt(count)
    factor = jnp.minimum(1.0, bound / jnp.sqrt(jnp.full((8, 128), total + EPS, jnp.float32)))
    panel = parts[0][...]
    for part in parts[1:]:
        panel = panel + part[...]
    panel = panel * factor[:1, :1]
    half = low_ref.shape[1]
    low_ref[...] = panel[:, :half]
    high_ref[...] = panel[:, half:]
    factor_ref[...] = factor


def clip(here, there, parts, count):
    rank, rows = parts[0].shape
    half = jax.ShapeDtypeStruct((rank, rows // 2), jnp.float32)
    return pl.pallas_call(
        functools.partial(clip_kernel, count=count),
        in_specs=[IN_VMEM] * (2 + len(parts)),
        out_specs=[IN_VMEM] * 3,
        out_shape=[half, half, jax.ShapeDtypeStruct((8, 128), jnp.float32)],
        compiler_params=KERNEL,
    )(here, there, *parts)


def core_parity():
    return lax.rem(lax.axis_index("shard"), 2)


def shard_columns(parity, j, width):
    return pl.ds(pl.multiple_of((2 * j + parity) * width, width), width)


def panel_of(parity, coeffs_ref, delta_ref, rows):
    total = None
    for j in range(CHIPS_Y):
        coeffs = jnp.concatenate([coeffs_ref[j, 0], coeffs_ref[j, 1]], axis=1)
        part = lax.dot_general(
            coeffs,
            delta_ref[rows, shard_columns(parity, j, coeffs.shape[1])],
            (((1,), (1,)), ((), ())),
            preferred_element_type=jnp.float32,
        )
        total = part if total is None else total + part
    return total


def total_energy(coeffs_ref):
    energy = 0.0
    for j in range(CHIPS_Y):
        for h in range(2):
            energy = energy + energy_of(coeffs_ref[j, h])
    return energy


def own_panel_kernel(coeffs_ref, delta_ref, panel_ref, energy_ref):
    panel_ref[...] = panel_of(core_parity(), coeffs_ref, delta_ref, slice(None))
    energy_ref[0, 0] = total_energy(coeffs_ref)


def own_panel(coeffs, mine):
    return pl.pallas_call(
        own_panel_kernel,
        in_specs=[IN_VMEM, IN_VMEM],
        out_specs=[IN_VMEM, IN_SMEM],
        out_shape=[jax.ShapeDtypeStruct((coeffs.shape[2], mine.shape[0]), jnp.float32), SCALAR],
        compiler_params=KERNEL,
    )(coeffs, mine)


def half_panel_kernel(coeffs_ref, delta_ref, factor_ref, own_ref, panel_ref, *energy_ref, high):
    half = panel_ref.shape[1]
    rows = slice(half, 2 * half) if high else slice(0, half)
    panel = panel_of(1 - core_parity(), coeffs_ref, delta_ref, rows)
    panel_ref[...] = (panel + own_ref[:, rows]) * factor_ref[:1, :1]
    for ref in energy_ref:
        ref[0, 0] = total_energy(coeffs_ref)


def half_panel(coeffs, mine, factor, own, high):
    shapes = [jax.ShapeDtypeStruct((own.shape[0], own.shape[1] // 2), jnp.float32)]
    specs = [IN_VMEM]
    if high:
        shapes.append(SCALAR)
        specs.append(IN_SMEM)
    return pl.pallas_call(
        functools.partial(half_panel_kernel, high=high),
        in_specs=[IN_VMEM] * 4,
        out_specs=specs,
        out_shape=shapes,
        compiler_params=KERNEL,
    )(coeffs, mine, factor, own)


def value_kernel(factor_ref, panel_ref, delta_ref, out_ref, *, own):
    parity = core_parity() if own else 1 - core_parity()
    half = out_ref.shape[-1]
    for j in range(CHIPS_Y):
        value = factor_ref[:1, :1] * lax.dot_general(
            panel_ref[...],
            delta_ref[:, shard_columns(parity, j, 2 * half)],
            (((1,), (0,)), ((), ())),
            preferred_element_type=jnp.float32,
        )
        value = value.astype(out_ref.dtype)
        out_ref[j, 0] = value[:, :half]
        out_ref[j, 1] = value[:, half:]


def value_part(panel, mine, factor, own, dtype):
    half = mine.shape[1] // (4 * CHIPS_Y)
    return pl.pallas_call(
        functools.partial(value_kernel, own=own),
        in_specs=[IN_VMEM, IN_VMEM, IN_VMEM],
        out_specs=IN_VMEM,
        out_shape=jax.ShapeDtypeStruct((CHIPS_Y, 2, panel.shape[0], half), dtype),
        compiler_params=KERNEL,
    )(factor, panel, mine)


def merge_kernel(blocks_ref, noise_ref, out_ref, *, step):
    client = lax.axis_index("client")
    total = jnp.zeros(blocks_ref.shape[1:], jnp.float32)
    for i in range(blocks_ref.shape[0]):
        total = total + blocks_ref[i].astype(jnp.float32)
    rows, half = total.shape
    row = pl.ds(pl.multiple_of(lax.div(client, 2) * rows, rows), rows)
    lane = pl.ds(pl.multiple_of(lax.rem(client, 2) * half, half), half)
    total = total + noise_ref[step, row, lane]
    out_ref[...] = jnp.broadcast_to(total.astype(out_ref.dtype), out_ref.shape)


def merge(blocks, noise, step, copies, dtype):
    return pl.pallas_call(
        functools.partial(merge_kernel, step=step),
        in_specs=[IN_VMEM, IN_VMEM],
        out_specs=IN_VMEM,
        out_shape=jax.ShapeDtypeStruct((copies,) + blocks.shape[1:], dtype),
        compiler_params=KERNEL,
    )(blocks, noise)


def gram_kernel(*refs, step, energies):
    parts, (low_ref, low_there, high_ref, high_there, noise_ref, panel_ref, gram_ref) = (
        refs[:energies],
        refs[energies:],
    )
    energy = parts[0][0, 0]
    for part in parts[1:]:
        energy = energy + part[0, 0]
    rank = panel_ref.shape[0]
    level = jnp.sqrt(jnp.full((8, 128), energy / rank, jnp.float32))[:1, :1]
    half = low_ref.shape[1]
    gram = None
    for i, (here, there) in enumerate(((low_ref, low_there), (high_ref, high_there))):
        rows = slice(i * half, (i + 1) * half)
        panel = (here[...] + there[...]) + level * noise_ref[step, :, rows]
        panel_ref[:, rows] = panel
        part = lax.dot_general(
            panel,
            panel,
            (((1,), (1,)), ((), ())),
            precision=lax.Precision.HIGHEST,
            preferred_element_type=jnp.float32,
        )
        gram = part if gram is None else gram + part
    gram = jnp.concatenate([gram[: rank // 2], gram[rank // 2 :]], axis=1)
    gram_ref[...] = jnp.broadcast_to(gram, gram_ref.shape)


def noisy_gram(energies, halves, noise, step):
    rank, rows = noise.shape[1:]
    return pl.pallas_call(
        functools.partial(gram_kernel, step=step, energies=len(energies)),
        in_specs=[IN_SMEM] * len(energies) + [IN_VMEM] * 5,
        out_specs=[IN_VMEM, IN_VMEM],
        out_shape=[
            jax.ShapeDtypeStruct((rank, rows), jnp.float32),
            jax.ShapeDtypeStruct((SHARDS, rank // 2, 2 * rank), jnp.float32),
        ],
        compiler_params=KERNEL,
    )(*energies, *halves, noise)


def inverse_factor(gram):
    rank = gram.shape[0]
    groups = rank // 8
    lane = lax.broadcasted_iota(jnp.int32, (8, 2 * rank), 1)
    row = lax.broadcasted_iota(jnp.int32, (8, 2 * rank), 0)

    def spread(tile, r):
        return jnp.broadcast_to(tile[r : r + 1, :], tile.shape)

    work = []
    for g in range(groups):
        right = jnp.concatenate(
            [jnp.zeros((8, rank), jnp.float32), gram[8 * g : 8 * g + 8, :]], axis=1
        )
        work.append(jnp.where(lane == row + 8 * g, 1.0, right))
    for b in range(groups):
        column = [
            [
                jnp.broadcast_to(
                    work[g][:, rank + 8 * b + j : rank + 8 * b + j + 1], (8, 2 * rank)
                )
                for g in range(b, groups)
            ]
            for j in range(8)
        ]
        diagonal = jnp.zeros((8, 2 * rank), jnp.float32)
        for j in range(8):
            pivot = spread(column[j][0], j)
            diagonal = jnp.where(row == j, pivot, diagonal)
            inverse = 1.0 / pivot
            ratio = [c * inverse for c in column[j]]
            ratio[0] = jnp.where(row > j, ratio[0], 0.0)
            for k in range(j + 1, 8):
                top = spread(column[k][0], j)
                column[k] = [c - f * top for c, f in zip(column[k], ratio)]
            top = spread(work[b], j)
            for g in range(b, groups):
                work[g] = work[g] - ratio[g - b] * top
        work[b] = work[b] * (1.0 / jnp.sqrt(diagonal))
    return jnp.concatenate([w[:, :rank] for w in work], axis=0)


def solve_kernel(gram_ref, panel_ref, rounded_ref, *basis_ref):
    gram = gram_ref[0]
    for i in range(1, gram_ref.shape[0]):
        gram = gram + gram_ref[i]
    rank = panel_ref.shape[0]
    gram = jnp.concatenate([gram[:, :rank], gram[:, rank:]], axis=0)
    panel = lax.dot_general(
        inverse_factor(gram),
        panel_ref[...],
        (((1,), (0,)), ((), ())),
        precision=lax.Precision.HIGHEST,
        preferred_element_type=jnp.float32,
    )
    rounded_ref[...] = panel.astype(rounded_ref.dtype)
    for ref in basis_ref:
        ref[...] = math.sqrt(D) * panel


def orthonormal(grams, panel, last):
    shapes = [jax.ShapeDtypeStruct(panel.shape, jnp.bfloat16)]
    if last:
        shapes.append(jax.ShapeDtypeStruct(panel.shape, jnp.float32))
    return pl.pallas_call(
        solve_kernel,
        in_specs=[IN_VMEM, IN_VMEM],
        out_specs=[IN_VMEM] * len(shapes),
        out_shape=shapes,
        compiler_params=KERNEL,
    )(grams, panel)


def on_device(delta, start_coeffs, noise_p, noise_q):
    coeffs = start_coeffs.T
    rank, columns = coeffs.shape
    panel_noise = noise_p.transpose(0, 2, 1)
    value_noise = noise_q.transpose(0, 2, 1)

    mine, squares = resident(delta[0])
    first, first_energy = first_panel(coeffs, mine, 0)
    second, second_energy = first_panel(coeffs, mine, 1)
    squares = squares + lax.ppermute(squares, "shard", SHARD_STEPS[0])
    squares = squares + lax.ppermute(squares, "shard", SHARD_STEPS[1])
    squares, first = lax.optimization_barrier((squares, first))
    parts = (first, second)
    energies = (first_energy, second_energy)
    there = lax.ppermute(squares, "shard", SHARD_STEPS[-1])
    low, high, factor = clip(squares, there, parts, D * columns)
    for step in range(ITERS):
        last = step + 1 == ITERS
        for low_pairs, high_pairs in CLIENT_STEPS[:-1]:
            low_there = lax.ppermute(low, "client", low_pairs)
            high_there = lax.ppermute(high, "client", high_pairs)
            low = low + low_there
            high = high + high_there
        low_pairs, high_pairs = CLIENT_STEPS[-1]
        low_there = lax.ppermute(low, "client", low_pairs)
        high_there = lax.ppermute(high, "client", high_pairs)
        halves = (low, low_there, high, high_there)
        panel, grams = noisy_gram(energies, halves, panel_noise, step)
        grams = lax.all_to_all(grams, "shard", 0, 0)
        rounded, *basis = orthonormal(grams, panel, last)
        away = value_part(rounded, mine, factor, False, jnp.bfloat16)
        away = lax.ppermute(away, "shard", CORE_SWAP)
        home = value_part(rounded, mine, factor, True, jnp.float32)
        chip = (home + away.astype(jnp.float32)).astype(jnp.bfloat16)
        blocks = chip.reshape(CHIPS_Y * CLIENTS, ROW_GROUP, chip.shape[-1])
        blocks = lax.all_to_all(
            blocks, ("client", "shard"), 0, 0, axis_index_groups=SAME_CORE
        )
        if last:
            value = merge(blocks, value_noise, step, CLIENTS, jnp.float32)
            value = lax.all_to_all(value, "client", 0, 0)
        else:
            same = merge(blocks, value_noise, step, CHIPS_Y * CLIENTS, jnp.bfloat16)
            same = lax.all_to_all(same, ("client", "shard"), 0, 0, axis_index_groups=SAME_CORE)
            same = same.reshape(chip.shape)
            other = lax.ppermute(same, "shard", CORE_SWAP)
            own, own_energy = own_panel(same, mine)
            (low,) = half_panel(other, mine, factor, own, False)
            high, other_energy = half_panel(other, mine, factor, own, True)
            energies = (own_energy, other_energy)
    half = value.shape[-1]
    value = value.reshape(rank // ROW_GROUP, 2, ROW_GROUP, half).transpose(0, 2, 1, 3)
    value = value.reshape(rank, 2 * half)
    return (basis[0].T, value.T)


def solution(mesh):
    placed = (P("client", "shard", None), P(), P(None, "shard", None), P(None, "shard", None))
    return jax.shard_map(
        on_device,
        mesh=mesh,
        in_specs=placed,
        out_specs=(P("shard", None), P("shard", None)),
        check_vma=False,
    )
```

```python
import functools
import math

import jax
import jax.numpy as jnp
from jax import lax
from jax.experimental import pallas as pl
from jax.experimental.pallas import tpu as pltpu
from jax.sharding import PartitionSpec as P

D = 4096
ITERS = 2
EPS = 1e-06
CLIP_FRACTION = 0.5

CLIENTS = 16
SHARDS = 8
CHIPS_Y = 4
ROW_GROUP = 8
FIRST_PARTS = 2

IN_VMEM = pl.BlockSpec(memory_space=pltpu.VMEM)
TILE = jax.ShapeDtypeStruct((8, 128), jnp.float32)
KERNEL = pltpu.CompilerParams(vmem_limit_bytes=16 << 20)


def client_pairs(even, odd):
    pairs = []
    for client in range(CLIENTS):
        for shard in range(SHARDS):
            flip_x, flip_z = odd if shard % 2 else even
            there = flip_x(client // 4) * 4 + flip_z(client % 4)
            pairs.append((client * SHARDS + shard, there * SHARDS + shard))
    return pairs


def keep(i):
    return i


def flip(i):
    return i ^ 1


def mirror(i):
    return 3 - i


ALONG_Z = ((keep, flip), (keep, mirror))
ALONG_X = ((flip, keep), (mirror, keep))
CLIENT_STEPS = [client_pairs(*ways) for ways in zip(ALONG_Z + ALONG_X, ALONG_X + ALONG_Z)]
CORE_SWAP = [(i, i ^ 1) for i in range(8)]
SHARD_STEPS = (
    CORE_SWAP,
    [(y * 2 + c, flip(y) * 2 + c) for y in range(4) for c in range(2)],
    [(y * 2 + c, mirror(y) * 2 + c) for y in range(4) for c in range(2)],
)
SAME_CORE = [
    [
        (g * 2 + h) * SHARDS + 2 * y + c
        for y in range(CHIPS_Y)
        for h in range(2)
        for g in range(CLIENTS // 2)
    ]
    for c in range(2)
]


def energy_of(coeffs):
    wide = coeffs.astype(jnp.float32)
    wide = (wide * wide).reshape(-1, 8, wide.shape[-1]).sum(0)
    total = wide[:, :128]
    for k in range(1, wide.shape[1] // 128):
        total = total + wide[:, k * 128 : (k + 1) * 128]
    return total


def resident_kernel(delta_hbm, delta_ref, squares_ref, sems):
    count = sems.shape[0]
    rows = delta_ref.shape[0] // count

    def copy(i):
        part = pl.ds(i * rows, rows)
        return pltpu.make_async_copy(delta_hbm.at[part, :], delta_ref.at[part, :], sems.at[i])

    for i in range(count):
        copy(i).start()
    total = jnp.zeros((8, 128), jnp.float32)
    for i in range(count):
        copy(i).wait()

        def column(c, total):
            part = delta_ref[pl.ds(i * rows, rows), pl.ds(pl.multiple_of(c * 1024, 1024), 1024)]
            part = part.astype(jnp.float32)
            return total + (part * part).reshape(rows // 8, 8, 1024).sum(0)

        wide = lax.fori_loop(
            0, delta_ref.shape[1] // 1024, column, jnp.zeros((8, 1024), jnp.float32), unroll=2
        )
        for k in range(8):
            total = total + wide[:, k * 128 : (k + 1) * 128]
    squares_ref[...] = total


def resident(mine, chunks=16):
    return pl.pallas_call(
        resident_kernel,
        in_specs=[pl.BlockSpec(memory_space=pltpu.HBM)],
        out_specs=[IN_VMEM, IN_VMEM],
        out_shape=[
            pltpu.VMEM(mine.shape, mine.dtype),
            jax.ShapeDtypeStruct((8, 128), jnp.float32),
        ],
        scratch_shapes=[pltpu.SemaphoreType.DMA((chunks,))],
        compiler_params=KERNEL,
    )(pltpu.with_memory_space_constraint(mine, pltpu.HBM))


def first_panel_kernel(coeffs_ref, delta_ref, panel_ref, energy_ref, *, part):
    width = coeffs_ref.shape[1] // FIRST_PARTS
    coeffs = coeffs_ref[:, part * width : (part + 1) * width]
    panel_ref[...] = lax.dot_general(
        coeffs,
        delta_ref[:, part * width : (part + 1) * width],
        (((1,), (1,)), ((), ())),
        preferred_element_type=jnp.float32,
    )
    energy_ref[...] = energy_of(coeffs)


def first_panel(coeffs, mine, part):
    return pl.pallas_call(
        functools.partial(first_panel_kernel, part=part),
        in_specs=[IN_VMEM, IN_VMEM],
        out_specs=[IN_VMEM, IN_VMEM],
        out_shape=[jax.ShapeDtypeStruct((coeffs.shape[0], mine.shape[0]), jnp.float32), TILE],
        compiler_params=KERNEL,
    )(coeffs, mine)


def clip_kernel(here_ref, there_ref, *refs, count):
    *parts, panel_ref, factor_ref = refs
    total = jnp.sum(here_ref[...] + there_ref[...])
    bound = CLIP_FRACTION * math.sqrt(count)
    factor = jnp.minimum(1.0, bound / jnp.sqrt(jnp.full((8, 128), total + EPS, jnp.float32)))
    panel = parts[0][...]
    for part in parts[1:]:
        panel = panel + part[...]
    panel_ref[...] = panel * factor[:1, :1]
    factor_ref[...] = factor


def clip(here, there, parts, count):
    return pl.pallas_call(
        functools.partial(clip_kernel, count=count),
        in_specs=[IN_VMEM] * (2 + len(parts)),
        out_specs=[IN_VMEM] * 2,
        out_shape=[jax.ShapeDtypeStruct(parts[0].shape, jnp.float32), TILE],
        compiler_params=KERNEL,
    )(here, there, *parts)


def core_parity():
    return lax.rem(lax.axis_index("shard"), 2)


def shard_columns(parity, j, width):
    return pl.ds(pl.multiple_of((2 * j + parity) * width, width), width)


def panel_of(parity, coeffs_ref, delta_ref):
    panel = None
    energy = jnp.zeros((8, 128), jnp.float32)
    for j in range(CHIPS_Y):
        coeffs = jnp.concatenate([coeffs_ref[j, 0], coeffs_ref[j, 1]], axis=1)
        part = lax.dot_general(
            coeffs,
            delta_ref[:, shard_columns(parity, j, coeffs.shape[1])],
            (((1,), (1,)), ((), ())),
            preferred_element_type=jnp.float32,
        )
        panel = part if panel is None else panel + part
        energy = energy + energy_of(coeffs)
    return panel, energy


def own_panel_kernel(coeffs_ref, delta_ref, panel_ref, energy_ref):
    panel_ref[...], energy_ref[...] = panel_of(core_parity(), coeffs_ref, delta_ref)


def whole_panel_kernel(coeffs_ref, delta_ref, factor_ref, own_ref, panel_ref, energy_ref):
    panel, energy_ref[...] = panel_of(1 - core_parity(), coeffs_ref, delta_ref)
    panel_ref[...] = (panel + own_ref[...]) * factor_ref[:1, :1]


def panel_part(kernel, coeffs, mine, *more):
    return pl.pallas_call(
        kernel,
        in_specs=[IN_VMEM] * (2 + len(more)),
        out_specs=[IN_VMEM, IN_VMEM],
        out_shape=[jax.ShapeDtypeStruct((coeffs.shape[2], mine.shape[0]), jnp.float32), TILE],
        compiler_params=KERNEL,
    )(coeffs, mine, *more)


def values_of(parity, factor_ref, panel_ref, delta_ref, out_ref):
    half = out_ref.shape[-1]
    for j in range(CHIPS_Y):
        value = factor_ref[:1, :1] * lax.dot_general(
            panel_ref[...],
            delta_ref[:, shard_columns(parity, j, 2 * half)],
            (((1,), (0,)), ((), ())),
            preferred_element_type=jnp.float32,
        )
        value = value.astype(out_ref.dtype)
        out_ref[j, 0] = value[:, :half]
        out_ref[j, 1] = value[:, half:]


def value_kernel(factor_ref, panel_ref, delta_ref, out_ref, *, own):
    parity = core_parity() if own else 1 - core_parity()
    values_of(parity, factor_ref, panel_ref, delta_ref, out_ref)


def value_store_kernel(factor_ref, panel_ref, delta_ref, basis_ref, out_ref, stored_ref, sem):
    copy = pltpu.make_async_copy(basis_ref, stored_ref, sem)
    copy.start()
    values_of(core_parity(), factor_ref, panel_ref, delta_ref, out_ref)
    copy.wait()


def value_shape(panel, mine, dtype):
    half = mine.shape[1] // (4 * CHIPS_Y)
    return jax.ShapeDtypeStruct((CHIPS_Y, 2, panel.shape[0], half), dtype)


def value_part(panel, mine, factor, own, dtype):
    return pl.pallas_call(
        functools.partial(value_kernel, own=own),
        in_specs=[IN_VMEM, IN_VMEM, IN_VMEM],
        out_specs=IN_VMEM,
        out_shape=value_shape(panel, mine, dtype),
        compiler_params=KERNEL,
    )(factor, panel, mine)


def value_store(panel, mine, factor, basis, dtype):
    return pl.pallas_call(
        value_store_kernel,
        in_specs=[IN_VMEM] * 4,
        out_specs=[IN_VMEM, pl.BlockSpec(memory_space=pltpu.HBM)],
        out_shape=[
            value_shape(panel, mine, dtype),
            jax.ShapeDtypeStruct(basis.shape, basis.dtype),
        ],
        scratch_shapes=[pltpu.SemaphoreType.DMA],
        compiler_params=KERNEL,
    )(factor, panel, mine, basis)


def merge_kernel(blocks_ref, noise_ref, out_ref, *, step):
    client = lax.axis_index("client")
    total = jnp.zeros(blocks_ref.shape[1:], jnp.float32)
    for i in range(blocks_ref.shape[0]):
        total = total + blocks_ref[i].astype(jnp.float32)
    rows, half = total.shape
    row = pl.ds(pl.multiple_of(lax.div(client, 2) * rows, rows), rows)
    lane = pl.ds(pl.multiple_of(lax.rem(client, 2) * half, half), half)
    total = total + noise_ref[step, row, lane]
    out_ref[...] = jnp.broadcast_to(total.astype(out_ref.dtype), out_ref.shape)


def merge(blocks, noise, step, copies, dtype):
    return pl.pallas_call(
        functools.partial(merge_kernel, step=step),
        in_specs=[IN_VMEM, IN_VMEM],
        out_specs=IN_VMEM,
        out_shape=jax.ShapeDtypeStruct((copies,) + blocks.shape[1:], dtype),
        compiler_params=KERNEL,
    )(blocks, noise)


def gram_kernel(first_ref, second_ref, here_ref, there_ref, noise_ref, panel_ref, gram_ref, *, step):
    rank = panel_ref.shape[0]
    energy = jnp.sum(first_ref[...] + second_ref[...])
    level = jnp.sqrt(jnp.full((8, 128), energy / rank, jnp.float32))[:1, :1]
    panel = (here_ref[...] + there_ref[...]) + level * noise_ref[step]
    panel_ref[...] = panel
    gram = lax.dot_general(
        panel,
        panel,
        (((1,), (1,)), ((), ())),
        precision=lax.Precision.HIGHEST,
        preferred_element_type=jnp.float32,
    )
    gram = jnp.concatenate([gram[: rank // 2], gram[rank // 2 :]], axis=1)
    gram_ref[...] = jnp.broadcast_to(gram, gram_ref.shape)


def noisy_gram(energies, here, there, noise, step):
    rank, rows = here.shape
    return pl.pallas_call(
        functools.partial(gram_kernel, step=step),
        in_specs=[IN_VMEM] * 5,
        out_specs=[IN_VMEM, IN_VMEM],
        out_shape=[
            jax.ShapeDtypeStruct((rank, rows), jnp.float32),
            jax.ShapeDtypeStruct((SHARDS, rank // 2, 2 * rank), jnp.float32),
        ],
        compiler_params=KERNEL,
    )(*energies, here, there, noise)


def inverse_factor(gram):
    rank = gram.shape[0]
    groups = rank // 8
    lane = lax.broadcasted_iota(jnp.int32, (8, 2 * rank), 1)
    row = lax.broadcasted_iota(jnp.int32, (8, 2 * rank), 0)

    def spread(tile, r):
        return jnp.broadcast_to(tile[r : r + 1, :], tile.shape)

    work = []
    for g in range(groups):
        right = jnp.concatenate(
            [jnp.zeros((8, rank), jnp.float32), gram[8 * g : 8 * g + 8, :]], axis=1
        )
        work.append(jnp.where(lane == row + 8 * g, 1.0, right))
    for b in range(groups):
        column = [
            [
                jnp.broadcast_to(
                    work[g][:, rank + 8 * b + j : rank + 8 * b + j + 1], (8, 2 * rank)
                )
                for g in range(b, groups)
            ]
            for j in range(8)
        ]
        diagonal = jnp.zeros((8, 2 * rank), jnp.float32)
        for j in range(8):
            pivot = spread(column[j][0], j)
            diagonal = jnp.where(row == j, pivot, diagonal)
            inverse = 1.0 / pivot
            ratio = [c * inverse for c in column[j]]
            ratio[0] = jnp.where(row > j, ratio[0], 0.0)
            for k in range(j + 1, 8):
                top = spread(column[k][0], j)
                column[k] = [c - f * top for c, f in zip(column[k], ratio)]
            top = spread(work[b], j)
            for g in range(b, groups):
                work[g] = work[g] - ratio[g - b] * top
        work[b] = work[b] * (1.0 / jnp.sqrt(diagonal))
    return jnp.concatenate([w[:, :rank] for w in work], axis=0)


def solve_kernel(gram_ref, panel_ref, rounded_ref, *basis_ref):
    gram = gram_ref[0]
    for i in range(1, gram_ref.shape[0]):
        gram = gram + gram_ref[i]
    rank = panel_ref.shape[0]
    gram = jnp.concatenate([gram[:, :rank], gram[:, rank:]], axis=0)
    panel = lax.dot_general(
        inverse_factor(gram),
        panel_ref[...],
        (((1,), (0,)), ((), ())),
        precision=lax.Precision.HIGHEST,
        preferred_element_type=jnp.float32,
    )
    rounded_ref[...] = panel.astype(rounded_ref.dtype)
    for ref in basis_ref:
        ref[...] = math.sqrt(D) * panel


def orthonormal(grams, panel, last):
    shapes = [jax.ShapeDtypeStruct(panel.shape, jnp.bfloat16)]
    if last:
        shapes.append(pltpu.VMEM(panel.shape, jnp.float32))
    return pl.pallas_call(
        solve_kernel,
        in_specs=[IN_VMEM, IN_VMEM],
        out_specs=[IN_VMEM] * len(shapes),
        out_shape=shapes,
        compiler_params=KERNEL,
    )(grams, panel)


def on_device(delta, start_coeffs, noise_p, noise_q):
    coeffs = start_coeffs.T
    rank, columns = coeffs.shape
    panel_noise = noise_p.transpose(0, 2, 1)
    value_noise = noise_q.transpose(0, 2, 1)

    mine, squares = resident(delta[0])
    first, first_energy = first_panel(coeffs, mine, 0)
    second, second_energy = first_panel(coeffs, mine, 1)
    squares = squares + lax.ppermute(squares, "shard", SHARD_STEPS[0])
    squares = squares + lax.ppermute(squares, "shard", SHARD_STEPS[1])
    squares, first = lax.optimization_barrier((squares, first))
    parts = (first, second)
    energies = (first_energy, second_energy)
    there = lax.ppermute(squares, "shard", SHARD_STEPS[-1])
    panel, factor = clip(squares, there, parts, D * columns)
    for step in range(ITERS):
        last = step + 1 == ITERS
        for pairs in CLIENT_STEPS[:-1]:
            panel = panel + lax.ppermute(panel, ("client", "shard"), pairs)
        there = lax.ppermute(panel, ("client", "shard"), CLIENT_STEPS[-1])
        panel, grams = noisy_gram(energies, panel, there, panel_noise, step)
        grams = lax.all_to_all(grams, "shard", 0, 0)
        rounded, *basis = orthonormal(grams, panel, last)
        away = value_part(rounded, mine, factor, False, jnp.bfloat16)
        away = lax.ppermute(away, "shard", CORE_SWAP)
        if last:
            home, basis = value_store(rounded, mine, factor, basis[0], jnp.float32)
        else:
            home = value_part(rounded, mine, factor, True, jnp.float32)
        chip = (home + away.astype(jnp.float32)).astype(jnp.bfloat16)
        blocks = chip.reshape(CHIPS_Y * CLIENTS, ROW_GROUP, chip.shape[-1])
        blocks = lax.all_to_all(
            blocks, ("client", "shard"), 0, 0, axis_index_groups=SAME_CORE
        )
        if last:
            value = merge(blocks, value_noise, step, CLIENTS, jnp.float32)
            value = lax.all_to_all(value, "client", 0, 0)
        else:
            same = merge(blocks, value_noise, step, CHIPS_Y * CLIENTS, jnp.bfloat16)
            same = lax.all_to_all(same, ("client", "shard"), 0, 0, axis_index_groups=SAME_CORE)
            same = same.reshape(chip.shape)
            other = lax.ppermute(same, "shard", CORE_SWAP)
            own, own_energy = panel_part(own_panel_kernel, same, mine)
            panel, other_energy = panel_part(whole_panel_kernel, other, mine, factor, own)
            energies = (own_energy, other_energy)
    half = value.shape[-1]
    value = value.reshape(rank // ROW_GROUP, 2, ROW_GROUP, half).transpose(0, 2, 1, 3)
    value = value.reshape(rank, 2 * half)
    return (basis.T, value.T)


def solution(mesh):
    placed = (P("client", "shard", None), P(), P(None, "shard", None), P(None, "shard", None))
    return jax.shard_map(
        on_device,
        mesh=mesh,
        in_specs=placed,
        out_specs=(P("shard", None), P("shard", None)),
        check_vma=False,
    )
```

```python
import functools
import math

import jax
import jax.numpy as jnp
from jax import lax
from jax.experimental import pallas as pl
from jax.experimental.pallas import tpu as pltpu
from jax.sharding import PartitionSpec as P

D = 4096
ITERS = 2
EPS = 1e-06
CLIP_FRACTION = 0.5

CLIENTS = 16
SHARDS = 8
CHIPS_Y = 4
ROW_GROUP = 8
FIRST_PARTS = 2

IN_VMEM = pl.BlockSpec(memory_space=pltpu.VMEM)
TILE = jax.ShapeDtypeStruct((8, 128), jnp.float32)
KERNEL = pltpu.CompilerParams(vmem_limit_bytes=16 << 20)


def client_pairs(even, odd):
    pairs = []
    for client in range(CLIENTS):
        for shard in range(SHARDS):
            flip_x, flip_z = odd if shard % 2 else even
            there = flip_x(client // 4) * 4 + flip_z(client % 4)
            pairs.append((client * SHARDS + shard, there * SHARDS + shard))
    return pairs


def keep(i):
    return i


def flip(i):
    return i ^ 1


def mirror(i):
    return 3 - i


def across(i):
    return (i + 2) % 4


WAYS = (across, flip, mirror)
CLIENT_ROUNDS = (
    [client_pairs((keep, way), (way, keep)) for way in WAYS],
    [client_pairs((way, keep), (keep, way)) for way in WAYS],
)
CORE_SWAP = [(i, i ^ 1) for i in range(8)]
SHARD_STEPS = (
    CORE_SWAP,
    [(y * 2 + c, flip(y) * 2 + c) for y in range(4) for c in range(2)],
    [(y * 2 + c, mirror(y) * 2 + c) for y in range(4) for c in range(2)],
)
SAME_CORE = [
    [
        (g * 2 + h) * SHARDS + 2 * y + c
        for y in range(CHIPS_Y)
        for h in range(2)
        for g in range(CLIENTS // 2)
    ]
    for c in range(2)
]


def energy_of(coeffs):
    wide = coeffs.astype(jnp.float32)
    wide = (wide * wide).reshape(-1, 8, wide.shape[-1]).sum(0)
    total = wide[:, :128]
    for k in range(1, wide.shape[1] // 128):
        total = total + wide[:, k * 128 : (k + 1) * 128]
    return total


def resident_kernel(delta_hbm, delta_ref, squares_ref, sems):
    count = sems.shape[0]
    rows = delta_ref.shape[0] // count

    def copy(i):
        part = pl.ds(i * rows, rows)
        return pltpu.make_async_copy(delta_hbm.at[part, :], delta_ref.at[part, :], sems.at[i])

    for i in range(count):
        copy(i).start()
    total = jnp.zeros((8, 128), jnp.float32)
    for i in range(count):
        copy(i).wait()

        def column(c, total):
            part = delta_ref[pl.ds(i * rows, rows), pl.ds(pl.multiple_of(c * 1024, 1024), 1024)]
            part = part.astype(jnp.float32)
            return total + (part * part).reshape(rows // 8, 8, 1024).sum(0)

        wide = lax.fori_loop(
            0, delta_ref.shape[1] // 1024, column, jnp.zeros((8, 1024), jnp.float32), unroll=2
        )
        for k in range(8):
            total = total + wide[:, k * 128 : (k + 1) * 128]
    squares_ref[...] = total


def resident(mine, chunks=16):
    return pl.pallas_call(
        resident_kernel,
        in_specs=[pl.BlockSpec(memory_space=pltpu.HBM)],
        out_specs=[IN_VMEM, IN_VMEM],
        out_shape=[
            pltpu.VMEM(mine.shape, mine.dtype),
            jax.ShapeDtypeStruct((8, 128), jnp.float32),
        ],
        scratch_shapes=[pltpu.SemaphoreType.DMA((chunks,))],
        compiler_params=KERNEL,
    )(pltpu.with_memory_space_constraint(mine, pltpu.HBM))


def first_panel_kernel(coeffs_ref, delta_ref, panel_ref, energy_ref, *, part):
    width = coeffs_ref.shape[1] // FIRST_PARTS
    coeffs = coeffs_ref[:, part * width : (part + 1) * width]
    panel_ref[...] = lax.dot_general(
        coeffs,
        delta_ref[:, part * width : (part + 1) * width],
        (((1,), (1,)), ((), ())),
        preferred_element_type=jnp.float32,
    )
    energy_ref[...] = energy_of(coeffs)


def first_panel(coeffs, mine, part):
    return pl.pallas_call(
        functools.partial(first_panel_kernel, part=part),
        in_specs=[IN_VMEM, IN_VMEM],
        out_specs=[IN_VMEM, IN_VMEM],
        out_shape=[jax.ShapeDtypeStruct((coeffs.shape[0], mine.shape[0]), jnp.float32), TILE],
        compiler_params=KERNEL,
    )(coeffs, mine)


def clip_kernel(here_ref, there_ref, *refs, count):
    *parts, panel_ref, factor_ref = refs
    total = jnp.sum(here_ref[...] + there_ref[...])
    bound = CLIP_FRACTION * math.sqrt(count)
    factor = jnp.minimum(1.0, bound / jnp.sqrt(jnp.full((8, 128), total + EPS, jnp.float32)))
    panel = parts[0][...]
    for part in parts[1:]:
        panel = panel + part[...]
    panel_ref[...] = panel * factor[:1, :1]
    factor_ref[...] = factor


def clip(here, there, parts, count):
    return pl.pallas_call(
        functools.partial(clip_kernel, count=count),
        in_specs=[IN_VMEM] * (2 + len(parts)),
        out_specs=[IN_VMEM] * 2,
        out_shape=[jax.ShapeDtypeStruct(parts[0].shape, jnp.float32), TILE],
        compiler_params=KERNEL,
    )(here, there, *parts)


def core_parity():
    return lax.rem(lax.axis_index("shard"), 2)


def shard_columns(parity, j, width):
    return pl.ds(pl.multiple_of((2 * j + parity) * width, width), width)


def panel_of(parity, coeffs_ref, delta_ref):
    panel = None
    energy = jnp.zeros((8, 128), jnp.float32)
    for j in range(CHIPS_Y):
        coeffs = jnp.concatenate([coeffs_ref[j, 0], coeffs_ref[j, 1]], axis=1)
        part = lax.dot_general(
            coeffs,
            delta_ref[:, shard_columns(parity, j, coeffs.shape[1])],
            (((1,), (1,)), ((), ())),
            preferred_element_type=jnp.float32,
        )
        panel = part if panel is None else panel + part
        energy = energy + energy_of(coeffs)
    return panel, energy


def own_panel_kernel(coeffs_ref, delta_ref, panel_ref, energy_ref):
    panel_ref[...], energy_ref[...] = panel_of(core_parity(), coeffs_ref, delta_ref)


def whole_panel_kernel(coeffs_ref, delta_ref, factor_ref, own_ref, panel_ref, energy_ref):
    panel, energy_ref[...] = panel_of(1 - core_parity(), coeffs_ref, delta_ref)
    panel_ref[...] = (panel + own_ref[...]) * factor_ref[:1, :1]


def panel_part(kernel, coeffs, mine, *more):
    return pl.pallas_call(
        kernel,
        in_specs=[IN_VMEM] * (2 + len(more)),
        out_specs=[IN_VMEM, IN_VMEM],
        out_shape=[jax.ShapeDtypeStruct((coeffs.shape[2], mine.shape[0]), jnp.float32), TILE],
        compiler_params=KERNEL,
    )(coeffs, mine, *more)


def values_of(parity, factor_ref, panel_ref, delta_ref, out_ref):
    half = out_ref.shape[-1]
    for j in range(CHIPS_Y):
        value = factor_ref[:1, :1] * lax.dot_general(
            panel_ref[...],
            delta_ref[:, shard_columns(parity, j, 2 * half)],
            (((1,), (0,)), ((), ())),
            preferred_element_type=jnp.float32,
        )
        value = value.astype(out_ref.dtype)
        out_ref[j, 0] = value[:, :half]
        out_ref[j, 1] = value[:, half:]


def value_kernel(factor_ref, panel_ref, delta_ref, out_ref, *, own):
    parity = core_parity() if own else 1 - core_parity()
    values_of(parity, factor_ref, panel_ref, delta_ref, out_ref)


def value_store_kernel(factor_ref, panel_ref, delta_ref, basis_ref, out_ref, stored_ref, sem):
    copy = pltpu.make_async_copy(basis_ref, stored_ref, sem)
    copy.start()
    values_of(core_parity(), factor_ref, panel_ref, delta_ref, out_ref)
    copy.wait()


def value_shape(panel, mine, dtype):
    half = mine.shape[1] // (4 * CHIPS_Y)
    return jax.ShapeDtypeStruct((CHIPS_Y, 2, panel.shape[0], half), dtype)


def value_part(panel, mine, factor, own, dtype):
    return pl.pallas_call(
        functools.partial(value_kernel, own=own),
        in_specs=[IN_VMEM, IN_VMEM, IN_VMEM],
        out_specs=IN_VMEM,
        out_shape=value_shape(panel, mine, dtype),
        compiler_params=KERNEL,
    )(factor, panel, mine)


def value_store(panel, mine, factor, basis, dtype):
    return pl.pallas_call(
        value_store_kernel,
        in_specs=[IN_VMEM] * 4,
        out_specs=[IN_VMEM, pl.BlockSpec(memory_space=pltpu.HBM)],
        out_shape=[
            value_shape(panel, mine, dtype),
            jax.ShapeDtypeStruct(basis.shape, basis.dtype),
        ],
        scratch_shapes=[pltpu.SemaphoreType.DMA],
        compiler_params=KERNEL,
    )(factor, panel, mine, basis)


def merge_kernel(blocks_ref, noise_ref, out_ref, *, step):
    client = lax.axis_index("client")
    total = jnp.zeros(blocks_ref.shape[1:], jnp.float32)
    for i in range(blocks_ref.shape[0]):
        total = total + blocks_ref[i].astype(jnp.float32)
    rows, half = total.shape
    row = pl.ds(pl.multiple_of(lax.div(client, 2) * rows, rows), rows)
    lane = pl.ds(pl.multiple_of(lax.rem(client, 2) * half, half), half)
    total = total + noise_ref[step, row, lane]
    out_ref[...] = jnp.broadcast_to(total.astype(out_ref.dtype), out_ref.shape)


def merge(blocks, noise, step, copies, dtype):
    return pl.pallas_call(
        functools.partial(merge_kernel, step=step),
        in_specs=[IN_VMEM, IN_VMEM],
        out_specs=IN_VMEM,
        out_shape=jax.ShapeDtypeStruct((copies,) + blocks.shape[1:], dtype),
        compiler_params=KERNEL,
    )(blocks, noise)


def ring_sum(here, across_there, flip_there, mirror_there):
    return (here + across_there) + (flip_there + mirror_there)


def gram_kernel(first_ref, second_ref, *refs, step):
    *rings, noise_ref, panel_ref, gram_ref = refs
    rank = panel_ref.shape[0]
    energy = jnp.sum(first_ref[...] + second_ref[...])
    level = jnp.sqrt(jnp.full((8, 128), energy / rank, jnp.float32))[:1, :1]
    panel = ring_sum(*(ref[...] for ref in rings)) + level * noise_ref[step]
    panel_ref[...] = panel
    gram = lax.dot_general(
        panel,
        panel,
        (((1,), (1,)), ((), ())),
        precision=lax.Precision.HIGHEST,
        preferred_element_type=jnp.float32,
    )
    gram = jnp.concatenate([gram[: rank // 2], gram[rank // 2 :]], axis=1)
    gram_ref[...] = jnp.broadcast_to(gram, gram_ref.shape)


def noisy_gram(energies, rings, noise, step):
    rank, rows = rings[0].shape
    return pl.pallas_call(
        functools.partial(gram_kernel, step=step),
        in_specs=[IN_VMEM] * (3 + len(rings)),
        out_specs=[IN_VMEM, IN_VMEM],
        out_shape=[
            jax.ShapeDtypeStruct((rank, rows), jnp.float32),
            jax.ShapeDtypeStruct((SHARDS, rank // 2, 2 * rank), jnp.float32),
        ],
        compiler_params=KERNEL,
    )(*energies, *rings, noise)


def inverse_factor(gram):
    rank = gram.shape[0]
    groups = rank // 8
    lane = lax.broadcasted_iota(jnp.int32, (8, 2 * rank), 1)
    row = lax.broadcasted_iota(jnp.int32, (8, 2 * rank), 0)

    def spread(tile, r):
        return jnp.broadcast_to(tile[r : r + 1, :], tile.shape)

    work = []
    for g in range(groups):
        right = jnp.concatenate(
            [jnp.zeros((8, rank), jnp.float32), gram[8 * g : 8 * g + 8, :]], axis=1
        )
        work.append(jnp.where(lane == row + 8 * g, 1.0, right))
    for b in range(groups):
        column = [
            [
                jnp.broadcast_to(
                    work[g][:, rank + 8 * b + j : rank + 8 * b + j + 1], (8, 2 * rank)
                )
                for g in range(b, groups)
            ]
            for j in range(8)
        ]
        diagonal = jnp.zeros((8, 2 * rank), jnp.float32)
        for j in range(8):
            pivot = spread(column[j][0], j)
            diagonal = jnp.where(row == j, pivot, diagonal)
            inverse = 1.0 / pivot
            ratio = [c * inverse for c in column[j]]
            ratio[0] = jnp.where(row > j, ratio[0], 0.0)
            for k in range(j + 1, 8):
                top = spread(column[k][0], j)
                column[k] = [c - f * top for c, f in zip(column[k], ratio)]
            top = spread(work[b], j)
            for g in range(b, groups):
                work[g] = work[g] - ratio[g - b] * top
        work[b] = work[b] * (1.0 / jnp.sqrt(diagonal))
    return jnp.concatenate([w[:, :rank] for w in work], axis=0)


def solve_kernel(gram_ref, panel_ref, rounded_ref, *basis_ref):
    gram = gram_ref[0]
    for i in range(1, gram_ref.shape[0]):
        gram = gram + gram_ref[i]
    rank = panel_ref.shape[0]
    gram = jnp.concatenate([gram[:, :rank], gram[:, rank:]], axis=0)
    panel = lax.dot_general(
        inverse_factor(gram),
        panel_ref[...],
        (((1,), (0,)), ((), ())),
        precision=lax.Precision.HIGHEST,
        preferred_element_type=jnp.float32,
    )
    rounded_ref[...] = panel.astype(rounded_ref.dtype)
    for ref in basis_ref:
        ref[...] = math.sqrt(D) * panel


def orthonormal(grams, panel, last):
    shapes = [jax.ShapeDtypeStruct(panel.shape, jnp.bfloat16)]
    if last:
        shapes.append(pltpu.VMEM(panel.shape, jnp.float32))
    return pl.pallas_call(
        solve_kernel,
        in_specs=[IN_VMEM, IN_VMEM],
        out_specs=[IN_VMEM] * len(shapes),
        out_shape=shapes,
        compiler_params=KERNEL,
    )(grams, panel)


def ring_parts(panel, ways):
    return [panel] + [lax.ppermute(panel, ("client", "shard"), pairs) for pairs in ways]


def on_device(delta, start_coeffs, noise_p, noise_q):
    coeffs = start_coeffs.T
    rank, columns = coeffs.shape
    panel_noise = noise_p.transpose(0, 2, 1)
    value_noise = noise_q.transpose(0, 2, 1)

    mine, squares = resident(delta[0])
    first, first_energy = first_panel(coeffs, mine, 0)
    second, second_energy = first_panel(coeffs, mine, 1)
    squares = squares + lax.ppermute(squares, "shard", SHARD_STEPS[0])
    squares = squares + lax.ppermute(squares, "shard", SHARD_STEPS[1])
    squares, first = lax.optimization_barrier((squares, first))
    parts = (first, second)
    energies = (first_energy, second_energy)
    there = lax.ppermute(squares, "shard", SHARD_STEPS[-1])
    panel, factor = clip(squares, there, parts, D * columns)
    for step in range(ITERS):
        last = step + 1 == ITERS
        panel = ring_sum(*ring_parts(panel, CLIENT_ROUNDS[0]))
        rings = ring_parts(panel, CLIENT_ROUNDS[1])
        panel, grams = noisy_gram(energies, rings, panel_noise, step)
        grams = lax.all_to_all(grams, "shard", 0, 0)
        rounded, *basis = orthonormal(grams, panel, last)
        away = value_part(rounded, mine, factor, False, jnp.bfloat16)
        away = lax.ppermute(away, "shard", CORE_SWAP)
        if last:
            home, basis = value_store(rounded, mine, factor, basis[0], jnp.float32)
        else:
            home = value_part(rounded, mine, factor, True, jnp.float32)
        chip = (home + away.astype(jnp.float32)).astype(jnp.bfloat16)
        blocks = chip.reshape(CHIPS_Y * CLIENTS, ROW_GROUP, chip.shape[-1])
        blocks = lax.all_to_all(
            blocks, ("client", "shard"), 0, 0, axis_index_groups=SAME_CORE
        )
        if last:
            value = merge(blocks, value_noise, step, CLIENTS, jnp.float32)
            value = lax.all_to_all(value, "client", 0, 0)
        else:
            same = merge(blocks, value_noise, step, CHIPS_Y * CLIENTS, jnp.bfloat16)
            same = lax.all_to_all(same, ("client", "shard"), 0, 0, axis_index_groups=SAME_CORE)
            same = same.reshape(chip.shape)
            other = lax.ppermute(same, "shard", CORE_SWAP)
            own, own_energy = panel_part(own_panel_kernel, same, mine)
            panel, other_energy = panel_part(whole_panel_kernel, other, mine, factor, own)
            energies = (own_energy, other_energy)
    half = value.shape[-1]
    value = value.reshape(rank // ROW_GROUP, 2, ROW_GROUP, half).transpose(0, 2, 1, 3)
    value = value.reshape(rank, 2 * half)
    return (basis.T, value.T)


def solution(mesh):
    placed = (P("client", "shard", None), P(), P(None, "shard", None), P(None, "shard", None))
    return jax.shard_map(
        on_device,
        mesh=mesh,
        in_specs=placed,
        out_specs=(P("shard", None), P("shard", None)),
        check_vma=False,
    )
```

```python
import functools
import math

import jax
import jax.numpy as jnp
from jax import lax
from jax.experimental import pallas as pl
from jax.experimental.pallas import tpu as pltpu
from jax.sharding import PartitionSpec as P

D = 4096
ITERS = 2
EPS = 1e-06
CLIP_FRACTION = 0.5

CLIENTS = 16
SHARDS = 8
CHIPS_Y = 4
ROW_GROUP = 8
FIRST_PARTS = 2

IN_VMEM = pl.BlockSpec(memory_space=pltpu.VMEM)
TILE = jax.ShapeDtypeStruct((8, 128), jnp.float32)
KERNEL = pltpu.CompilerParams(vmem_limit_bytes=16 << 20)


def client_pairs(even, odd):
    pairs = []
    for client in range(CLIENTS):
        for shard in range(SHARDS):
            flip_x, flip_z = odd if shard % 2 else even
            there = flip_x(client // 4) * 4 + flip_z(client % 4)
            pairs.append((client * SHARDS + shard, there * SHARDS + shard))
    return pairs


def keep(i):
    return i


def flip(i):
    return i ^ 1


def mirror(i):
    return 3 - i


def across(i):
    return (i + 2) % 4


WAYS = (flip, mirror, across)
CLIENT_ROUNDS = (
    [client_pairs((keep, way), (way, keep)) for way in WAYS],
    [client_pairs((way, keep), (keep, way)) for way in WAYS],
)
CORE_SWAP = [(i, i ^ 1) for i in range(8)]
SHARD_STEPS = (
    CORE_SWAP,
    [(y * 2 + c, flip(y) * 2 + c) for y in range(4) for c in range(2)],
    [(y * 2 + c, mirror(y) * 2 + c) for y in range(4) for c in range(2)],
)
SAME_CORE = [
    [
        (g * 2 + h) * SHARDS + 2 * y + c
        for y in range(CHIPS_Y)
        for h in range(2)
        for g in range(CLIENTS // 2)
    ]
    for c in range(2)
]


def energy_of(coeffs):
    wide = coeffs.astype(jnp.float32)
    wide = (wide * wide).reshape(-1, 8, wide.shape[-1]).sum(0)
    total = wide[:, :128]
    for k in range(1, wide.shape[1] // 128):
        total = total + wide[:, k * 128 : (k + 1) * 128]
    return total


def resident_kernel(delta_hbm, delta_ref, squares_ref, sems):
    count = sems.shape[0]
    rows = delta_ref.shape[0] // count

    def copy(i):
        part = pl.ds(i * rows, rows)
        return pltpu.make_async_copy(delta_hbm.at[part, :], delta_ref.at[part, :], sems.at[i])

    for i in range(count):
        copy(i).start()
    total = jnp.zeros((8, 128), jnp.float32)
    for i in range(count):
        copy(i).wait()

        def column(c, total):
            part = delta_ref[pl.ds(i * rows, rows), pl.ds(pl.multiple_of(c * 1024, 1024), 1024)]
            part = part.astype(jnp.float32)
            return total + (part * part).reshape(rows // 8, 8, 1024).sum(0)

        wide = lax.fori_loop(
            0, delta_ref.shape[1] // 1024, column, jnp.zeros((8, 1024), jnp.float32), unroll=2
        )
        for k in range(8):
            total = total + wide[:, k * 128 : (k + 1) * 128]
    squares_ref[...] = total


def resident(mine, chunks=16):
    return pl.pallas_call(
        resident_kernel,
        in_specs=[pl.BlockSpec(memory_space=pltpu.HBM)],
        out_specs=[IN_VMEM, IN_VMEM],
        out_shape=[
            pltpu.VMEM(mine.shape, mine.dtype),
            jax.ShapeDtypeStruct((8, 128), jnp.float32),
        ],
        scratch_shapes=[pltpu.SemaphoreType.DMA((chunks,))],
        compiler_params=KERNEL,
    )(pltpu.with_memory_space_constraint(mine, pltpu.HBM))


def first_panel_kernel(coeffs_ref, delta_ref, panel_ref, energy_ref, *, part):
    width = coeffs_ref.shape[1] // FIRST_PARTS
    coeffs = coeffs_ref[:, part * width : (part + 1) * width]
    panel_ref[...] = lax.dot_general(
        coeffs,
        delta_ref[:, part * width : (part + 1) * width],
        (((1,), (1,)), ((), ())),
        preferred_element_type=jnp.float32,
    )
    energy_ref[...] = energy_of(coeffs)


def first_panel(coeffs, mine, part):
    return pl.pallas_call(
        functools.partial(first_panel_kernel, part=part),
        in_specs=[IN_VMEM, IN_VMEM],
        out_specs=[IN_VMEM, IN_VMEM],
        out_shape=[jax.ShapeDtypeStruct((coeffs.shape[0], mine.shape[0]), jnp.float32), TILE],
        compiler_params=KERNEL,
    )(coeffs, mine)


def clip_kernel(here_ref, there_ref, *refs, count):
    *parts, panel_ref, factor_ref = refs
    total = jnp.sum(here_ref[...] + there_ref[...])
    bound = CLIP_FRACTION * math.sqrt(count)
    factor = jnp.minimum(1.0, bound / jnp.sqrt(jnp.full((8, 128), total + EPS, jnp.float32)))
    panel = parts[0][...]
    for part in parts[1:]:
        panel = panel + part[...]
    panel_ref[...] = panel * factor[:1, :1]
    factor_ref[...] = factor


def clip(here, there, parts, count):
    return pl.pallas_call(
        functools.partial(clip_kernel, count=count),
        in_specs=[IN_VMEM] * (2 + len(parts)),
        out_specs=[IN_VMEM] * 2,
        out_shape=[jax.ShapeDtypeStruct(parts[0].shape, jnp.float32), TILE],
        compiler_params=KERNEL,
    )(here, there, *parts)


def core_parity():
    return lax.rem(lax.axis_index("shard"), 2)


def shard_columns(parity, j, width):
    return pl.ds(pl.multiple_of((2 * j + parity) * width, width), width)


def panel_of(parity, coeffs_ref, delta_ref):
    panel = None
    energy = jnp.zeros((8, 128), jnp.float32)
    for j in range(CHIPS_Y):
        coeffs = jnp.concatenate([coeffs_ref[j, 0], coeffs_ref[j, 1]], axis=1)
        part = lax.dot_general(
            coeffs,
            delta_ref[:, shard_columns(parity, j, coeffs.shape[1])],
            (((1,), (1,)), ((), ())),
            preferred_element_type=jnp.float32,
        )
        panel = part if panel is None else panel + part
        energy = energy + energy_of(coeffs)
    return panel, energy


def own_panel_kernel(coeffs_ref, delta_ref, panel_ref, energy_ref):
    panel_ref[...], energy_ref[...] = panel_of(core_parity(), coeffs_ref, delta_ref)


def whole_panel_kernel(coeffs_ref, delta_ref, factor_ref, own_ref, panel_ref, energy_ref):
    panel, energy_ref[...] = panel_of(1 - core_parity(), coeffs_ref, delta_ref)
    panel_ref[...] = (panel + own_ref[...]) * factor_ref[:1, :1]


def panel_part(kernel, coeffs, mine, *more):
    return pl.pallas_call(
        kernel,
        in_specs=[IN_VMEM] * (2 + len(more)),
        out_specs=[IN_VMEM, IN_VMEM],
        out_shape=[jax.ShapeDtypeStruct((coeffs.shape[2], mine.shape[0]), jnp.float32), TILE],
        compiler_params=KERNEL,
    )(coeffs, mine, *more)


def values_of(parity, factor_ref, panel_ref, delta_ref, out_ref):
    half = out_ref.shape[-1]
    for j in range(CHIPS_Y):
        value = factor_ref[:1, :1] * lax.dot_general(
            panel_ref[...],
            delta_ref[:, shard_columns(parity, j, 2 * half)],
            (((1,), (0,)), ((), ())),
            preferred_element_type=jnp.float32,
        )
        value = value.astype(out_ref.dtype)
        out_ref[j, 0] = value[:, :half]
        out_ref[j, 1] = value[:, half:]


def value_kernel(factor_ref, panel_ref, delta_ref, out_ref, *, own):
    parity = core_parity() if own else 1 - core_parity()
    values_of(parity, factor_ref, panel_ref, delta_ref, out_ref)


def value_store_kernel(factor_ref, panel_ref, delta_ref, basis_ref, out_ref, stored_ref, sem):
    copy = pltpu.make_async_copy(basis_ref, stored_ref, sem)
    copy.start()
    values_of(core_parity(), factor_ref, panel_ref, delta_ref, out_ref)
    copy.wait()


def value_shape(panel, mine, dtype):
    half = mine.shape[1] // (4 * CHIPS_Y)
    return jax.ShapeDtypeStruct((CHIPS_Y, 2, panel.shape[0], half), dtype)


def value_part(panel, mine, factor, own, dtype):
    return pl.pallas_call(
        functools.partial(value_kernel, own=own),
        in_specs=[IN_VMEM, IN_VMEM, IN_VMEM],
        out_specs=IN_VMEM,
        out_shape=value_shape(panel, mine, dtype),
        compiler_params=KERNEL,
    )(factor, panel, mine)


def value_store(panel, mine, factor, basis, dtype):
    return pl.pallas_call(
        value_store_kernel,
        in_specs=[IN_VMEM] * 4,
        out_specs=[IN_VMEM, pl.BlockSpec(memory_space=pltpu.HBM)],
        out_shape=[
            value_shape(panel, mine, dtype),
            jax.ShapeDtypeStruct(basis.shape, basis.dtype),
        ],
        scratch_shapes=[pltpu.SemaphoreType.DMA],
        compiler_params=KERNEL,
    )(factor, panel, mine, basis)


def merge_kernel(blocks_ref, noise_ref, out_ref, *, step):
    client = lax.axis_index("client")
    total = jnp.zeros(blocks_ref.shape[1:], jnp.float32)
    for i in range(blocks_ref.shape[0]):
        total = total + blocks_ref[i].astype(jnp.float32)
    rows, half = total.shape
    row = pl.ds(pl.multiple_of(lax.div(client, 2) * rows, rows), rows)
    lane = pl.ds(pl.multiple_of(lax.rem(client, 2) * half, half), half)
    total = total + noise_ref[step, row, lane]
    out_ref[...] = jnp.broadcast_to(total.astype(out_ref.dtype), out_ref.shape)


def merge(blocks, noise, step, copies, dtype):
    return pl.pallas_call(
        functools.partial(merge_kernel, step=step),
        in_specs=[IN_VMEM, IN_VMEM],
        out_specs=IN_VMEM,
        out_shape=jax.ShapeDtypeStruct((copies,) + blocks.shape[1:], dtype),
        compiler_params=KERNEL,
    )(blocks, noise)


def ring_sum(here, flip_there, mirror_there, across_there):
    return (flip_there + mirror_there) + (here + across_there)


def gram_kernel(first_ref, second_ref, *refs, step):
    *rings, noise_ref, panel_ref, gram_ref = refs
    rank = panel_ref.shape[0]
    energy = jnp.sum(first_ref[...] + second_ref[...])
    level = jnp.sqrt(jnp.full((8, 128), energy / rank, jnp.float32))[:1, :1]
    panel = ring_sum(*(ref[...] for ref in rings)) + level * noise_ref[step]
    panel_ref[...] = panel
    gram = lax.dot_general(
        panel,
        panel,
        (((1,), (1,)), ((), ())),
        precision=lax.Precision.HIGHEST,
        preferred_element_type=jnp.float32,
    )
    gram = jnp.concatenate([gram[: rank // 2], gram[rank // 2 :]], axis=1)
    gram_ref[...] = jnp.broadcast_to(gram, gram_ref.shape)


def noisy_gram(energies, rings, noise, step):
    rank, rows = rings[0].shape
    return pl.pallas_call(
        functools.partial(gram_kernel, step=step),
        in_specs=[IN_VMEM] * (3 + len(rings)),
        out_specs=[IN_VMEM, IN_VMEM],
        out_shape=[
            jax.ShapeDtypeStruct((rank, rows), jnp.float32),
            jax.ShapeDtypeStruct((SHARDS, rank // 2, 2 * rank), jnp.float32),
        ],
        compiler_params=KERNEL,
    )(*energies, *rings, noise)


def inverse_factor(gram):
    rank = gram.shape[0]
    groups = rank // 8
    lane = lax.broadcasted_iota(jnp.int32, (8, 2 * rank), 1)
    row = lax.broadcasted_iota(jnp.int32, (8, 2 * rank), 0)

    def spread(tile, r):
        return jnp.broadcast_to(tile[r : r + 1, :], tile.shape)

    work = []
    for g in range(groups):
        right = jnp.concatenate(
            [jnp.zeros((8, rank), jnp.float32), gram[8 * g : 8 * g + 8, :]], axis=1
        )
        work.append(jnp.where(lane == row + 8 * g, 1.0, right))
    for b in range(groups):
        column = [
            [
                jnp.broadcast_to(
                    work[g][:, rank + 8 * b + j : rank + 8 * b + j + 1], (8, 2 * rank)
                )
                for g in range(b, groups)
            ]
            for j in range(8)
        ]
        diagonal = jnp.zeros((8, 2 * rank), jnp.float32)
        for j in range(8):
            pivot = spread(column[j][0], j)
            diagonal = jnp.where(row == j, pivot, diagonal)
            inverse = 1.0 / pivot
            ratio = [c * inverse for c in column[j]]
            ratio[0] = jnp.where(row > j, ratio[0], 0.0)
            for k in range(j + 1, 8):
                top = spread(column[k][0], j)
                column[k] = [c - f * top for c, f in zip(column[k], ratio)]
            top = spread(work[b], j)
            for g in range(b, groups):
                work[g] = work[g] - ratio[g - b] * top
        work[b] = work[b] * (1.0 / jnp.sqrt(diagonal))
    return jnp.concatenate([w[:, :rank] for w in work], axis=0)


def solve_kernel(gram_ref, panel_ref, rounded_ref, *basis_ref):
    gram = gram_ref[0]
    for i in range(1, gram_ref.shape[0]):
        gram = gram + gram_ref[i]
    rank = panel_ref.shape[0]
    gram = jnp.concatenate([gram[:, :rank], gram[:, rank:]], axis=0)
    panel = lax.dot_general(
        inverse_factor(gram),
        panel_ref[...],
        (((1,), (0,)), ((), ())),
        precision=lax.Precision.HIGHEST,
        preferred_element_type=jnp.float32,
    )
    rounded_ref[...] = panel.astype(rounded_ref.dtype)
    for ref in basis_ref:
        ref[...] = math.sqrt(D) * panel


def orthonormal(grams, panel, last):
    shapes = [jax.ShapeDtypeStruct(panel.shape, jnp.bfloat16)]
    if last:
        shapes.append(pltpu.VMEM(panel.shape, jnp.float32))
    return pl.pallas_call(
        solve_kernel,
        in_specs=[IN_VMEM, IN_VMEM],
        out_specs=[IN_VMEM] * len(shapes),
        out_shape=shapes,
        compiler_params=KERNEL,
    )(grams, panel)


def ring_parts(panel, ways):
    return [panel] + [lax.ppermute(panel, ("client", "shard"), pairs) for pairs in ways]


def on_device(delta, start_coeffs, noise_p, noise_q):
    coeffs = start_coeffs.T
    rank, columns = coeffs.shape
    panel_noise = noise_p.transpose(0, 2, 1)
    value_noise = noise_q.transpose(0, 2, 1)

    mine, squares = resident(delta[0])
    first, first_energy = first_panel(coeffs, mine, 0)
    second, second_energy = first_panel(coeffs, mine, 1)
    squares = squares + lax.ppermute(squares, "shard", SHARD_STEPS[0])
    squares = squares + lax.ppermute(squares, "shard", SHARD_STEPS[1])
    squares, first = lax.optimization_barrier((squares, first))
    parts = (first, second)
    energies = (first_energy, second_energy)
    there = lax.ppermute(squares, "shard", SHARD_STEPS[-1])
    panel, factor = clip(squares, there, parts, D * columns)
    for step in range(ITERS):
        last = step + 1 == ITERS
        panel = ring_sum(*ring_parts(panel, CLIENT_ROUNDS[0]))
        rings = ring_parts(panel, CLIENT_ROUNDS[1])
        panel, grams = noisy_gram(energies, rings, panel_noise, step)
        grams = lax.all_to_all(grams, "shard", 0, 0)
        rounded, *basis = orthonormal(grams, panel, last)
        away = value_part(rounded, mine, factor, False, jnp.bfloat16)
        away = lax.ppermute(away, "shard", CORE_SWAP)
        if last:
            home, basis = value_store(rounded, mine, factor, basis[0], jnp.float32)
        else:
            home = value_part(rounded, mine, factor, True, jnp.float32)
        chip = (home + away.astype(jnp.float32)).astype(jnp.bfloat16)
        blocks = chip.reshape(CHIPS_Y * CLIENTS, ROW_GROUP, chip.shape[-1])
        blocks = lax.all_to_all(
            blocks, ("client", "shard"), 0, 0, axis_index_groups=SAME_CORE
        )
        if last:
            value = merge(blocks, value_noise, step, CLIENTS, jnp.float32)
            value = lax.all_to_all(value, "client", 0, 0)
        else:
            same = merge(blocks, value_noise, step, CHIPS_Y * CLIENTS, jnp.bfloat16)
            same = lax.all_to_all(same, ("client", "shard"), 0, 0, axis_index_groups=SAME_CORE)
            same = same.reshape(chip.shape)
            other = lax.ppermute(same, "shard", CORE_SWAP)
            own, own_energy = panel_part(own_panel_kernel, same, mine)
            panel, other_energy = panel_part(whole_panel_kernel, other, mine, factor, own)
            energies = (own_energy, other_energy)
    half = value.shape[-1]
    value = value.reshape(rank // ROW_GROUP, 2, ROW_GROUP, half).transpose(0, 2, 1, 3)
    value = value.reshape(rank, 2 * half)
    return (basis.T, value.T)


def solution(mesh):
    placed = (P("client", "shard", None), P(), P(None, "shard", None), P(None, "shard", None))
    return jax.shard_map(
        on_device,
        mesh=mesh,
        in_specs=placed,
        out_specs=(P("shard", None), P("shard", None)),
        check_vma=False,
    )
```

```python
import functools
import math

import jax
import jax.numpy as jnp
from jax import lax
from jax.experimental import pallas as pl
from jax.experimental.pallas import tpu as pltpu
from jax.sharding import PartitionSpec as P

D = 4096
ITERS = 2
EPS = 1e-06
CLIP_FRACTION = 0.5

CLIENTS = 16
SHARDS = 8
CHIPS_Y = 4
ROW_GROUP = 8
FIRST_PARTS = 2

IN_VMEM = pl.BlockSpec(memory_space=pltpu.VMEM)
TILE = jax.ShapeDtypeStruct((8, 128), jnp.float32)
KERNEL = pltpu.CompilerParams(vmem_limit_bytes=16 << 20)


def client_pairs(even, odd):
    pairs = []
    for client in range(CLIENTS):
        for shard in range(SHARDS):
            flip_x, flip_z = odd if shard % 2 else even
            there = flip_x(client // 4) * 4 + flip_z(client % 4)
            pairs.append((client * SHARDS + shard, there * SHARDS + shard))
    return pairs


def keep(i):
    return i


def flip(i):
    return i ^ 1


def mirror(i):
    return 3 - i


def across(i):
    return (i + 2) % 4


WAYS = (flip, mirror, across)
CLIENT_ROUNDS = (
    [client_pairs((keep, way), (way, keep)) for way in WAYS],
    [client_pairs((way, keep), (keep, way)) for way in WAYS],
)
CORE_SWAP = [(i, i ^ 1) for i in range(8)]
SHARD_STEPS = (
    CORE_SWAP,
    [(y * 2 + c, flip(y) * 2 + c) for y in range(4) for c in range(2)],
    [(y * 2 + c, mirror(y) * 2 + c) for y in range(4) for c in range(2)],
)
SAME_CORE = [
    [
        (g * 2 + h) * SHARDS + 2 * y + c
        for y in range(CHIPS_Y)
        for h in range(2)
        for g in range(CLIENTS // 2)
    ]
    for c in range(2)
]


def energy_of(coeffs):
    wide = coeffs.astype(jnp.float32)
    wide = (wide * wide).reshape(-1, 8, wide.shape[-1]).sum(0)
    total = wide[:, :128]
    for k in range(1, wide.shape[1] // 128):
        total = total + wide[:, k * 128 : (k + 1) * 128]
    return total


def resident_kernel(delta_hbm, delta_ref, squares_ref, sems):
    count = sems.shape[0]
    rows = delta_ref.shape[0] // count

    def copy(i):
        part = pl.ds(i * rows, rows)
        return pltpu.make_async_copy(delta_hbm.at[part, :], delta_ref.at[part, :], sems.at[i])

    for i in range(count):
        copy(i).start()
    total = jnp.zeros((8, 128), jnp.float32)
    for i in range(count):
        copy(i).wait()

        def column(c, total):
            part = delta_ref[pl.ds(i * rows, rows), pl.ds(pl.multiple_of(c * 1024, 1024), 1024)]
            part = part.astype(jnp.float32)
            return total + (part * part).reshape(rows // 8, 8, 1024).sum(0)

        wide = lax.fori_loop(
            0, delta_ref.shape[1] // 1024, column, jnp.zeros((8, 1024), jnp.float32), unroll=2
        )
        for k in range(8):
            total = total + wide[:, k * 128 : (k + 1) * 128]
    squares_ref[...] = total


def resident(mine, chunks=16):
    return pl.pallas_call(
        resident_kernel,
        in_specs=[pl.BlockSpec(memory_space=pltpu.HBM)],
        out_specs=[IN_VMEM, IN_VMEM],
        out_shape=[
            pltpu.VMEM(mine.shape, mine.dtype),
            jax.ShapeDtypeStruct((8, 128), jnp.float32),
        ],
        scratch_shapes=[pltpu.SemaphoreType.DMA((chunks,))],
        compiler_params=KERNEL,
    )(pltpu.with_memory_space_constraint(mine, pltpu.HBM))


def first_panel_kernel(coeffs_ref, delta_ref, panel_ref, energy_ref, *, part):
    width = coeffs_ref.shape[1] // FIRST_PARTS
    coeffs = coeffs_ref[:, part * width : (part + 1) * width]
    panel_ref[...] = lax.dot_general(
        coeffs,
        delta_ref[:, part * width : (part + 1) * width],
        (((1,), (1,)), ((), ())),
        preferred_element_type=jnp.float32,
    )
    energy_ref[...] = energy_of(coeffs)


def first_panel(coeffs, mine, part):
    return pl.pallas_call(
        functools.partial(first_panel_kernel, part=part),
        in_specs=[IN_VMEM, IN_VMEM],
        out_specs=[IN_VMEM, IN_VMEM],
        out_shape=[jax.ShapeDtypeStruct((coeffs.shape[0], mine.shape[0]), jnp.float32), TILE],
        compiler_params=KERNEL,
    )(coeffs, mine)


def clip_kernel(here_ref, there_ref, *refs, count):
    *parts, panel_ref, factor_ref = refs
    total = jnp.sum(here_ref[...] + there_ref[...])
    bound = CLIP_FRACTION * math.sqrt(count)
    factor = jnp.minimum(1.0, bound / jnp.sqrt(jnp.full((8, 128), total + EPS, jnp.float32)))
    panel = parts[0][...]
    for part in parts[1:]:
        panel = panel + part[...]
    panel_ref[...] = panel * factor[:1, :1]
    factor_ref[...] = factor


def clip(here, there, parts, count):
    return pl.pallas_call(
        functools.partial(clip_kernel, count=count),
        in_specs=[IN_VMEM] * (2 + len(parts)),
        out_specs=[IN_VMEM] * 2,
        out_shape=[jax.ShapeDtypeStruct(parts[0].shape, jnp.float32), TILE],
        compiler_params=KERNEL,
    )(here, there, *parts)


def core_parity():
    return lax.rem(lax.axis_index("shard"), 2)


def shard_columns(parity, j, width):
    return pl.ds(pl.multiple_of((2 * j + parity) * width, width), width)


def panel_of(parity, coeffs_ref, delta_ref):
    panel = None
    energy = jnp.zeros((8, 128), jnp.float32)
    for j in range(CHIPS_Y):
        coeffs = jnp.concatenate([coeffs_ref[j, 0], coeffs_ref[j, 1]], axis=1)
        part = lax.dot_general(
            coeffs,
            delta_ref[:, shard_columns(parity, j, coeffs.shape[1])],
            (((1,), (1,)), ((), ())),
            preferred_element_type=jnp.float32,
        )
        panel = part if panel is None else panel + part
        energy = energy + energy_of(coeffs)
    return panel, energy


def own_panel_kernel(coeffs_ref, delta_ref, panel_ref, energy_ref):
    panel_ref[...], energy_ref[...] = panel_of(core_parity(), coeffs_ref, delta_ref)


def whole_panel_kernel(coeffs_ref, delta_ref, factor_ref, own_ref, panel_ref, energy_ref):
    panel, energy_ref[...] = panel_of(1 - core_parity(), coeffs_ref, delta_ref)
    panel_ref[...] = (panel + own_ref[...]) * factor_ref[:1, :1]


def panel_part(kernel, coeffs, mine, *more):
    return pl.pallas_call(
        kernel,
        in_specs=[IN_VMEM] * (2 + len(more)),
        out_specs=[IN_VMEM, IN_VMEM],
        out_shape=[jax.ShapeDtypeStruct((coeffs.shape[2], mine.shape[0]), jnp.float32), TILE],
        compiler_params=KERNEL,
    )(coeffs, mine, *more)


def values_of(parity, factor_ref, panel_ref, delta_ref, out_ref):
    half = out_ref.shape[-1]
    for j in range(CHIPS_Y):
        value = factor_ref[:1, :1] * lax.dot_general(
            panel_ref[...],
            delta_ref[:, shard_columns(parity, j, 2 * half)],
            (((1,), (0,)), ((), ())),
            preferred_element_type=jnp.float32,
        )
        value = value.astype(out_ref.dtype)
        out_ref[j, 0] = value[:, :half]
        out_ref[j, 1] = value[:, half:]


def value_kernel(factor_ref, panel_ref, delta_ref, out_ref, *, own):
    parity = core_parity() if own else 1 - core_parity()
    values_of(parity, factor_ref, panel_ref, delta_ref, out_ref)


def value_store_kernel(factor_ref, panel_ref, delta_ref, basis_ref, out_ref, stored_ref, sem):
    copy = pltpu.make_async_copy(basis_ref, stored_ref, sem)
    copy.start()
    values_of(core_parity(), factor_ref, panel_ref, delta_ref, out_ref)
    copy.wait()


def value_shape(panel, mine, dtype):
    half = mine.shape[1] // (4 * CHIPS_Y)
    return jax.ShapeDtypeStruct((CHIPS_Y, 2, panel.shape[0], half), dtype)


def value_part(panel, mine, factor, own, dtype):
    return pl.pallas_call(
        functools.partial(value_kernel, own=own),
        in_specs=[IN_VMEM, IN_VMEM, IN_VMEM],
        out_specs=IN_VMEM,
        out_shape=value_shape(panel, mine, dtype),
        compiler_params=KERNEL,
    )(factor, panel, mine)


def value_store(panel, mine, factor, basis, dtype):
    return pl.pallas_call(
        value_store_kernel,
        in_specs=[IN_VMEM] * 4,
        out_specs=[IN_VMEM, pl.BlockSpec(memory_space=pltpu.HBM)],
        out_shape=[
            value_shape(panel, mine, dtype),
            jax.ShapeDtypeStruct(basis.shape, basis.dtype),
        ],
        scratch_shapes=[pltpu.SemaphoreType.DMA],
        compiler_params=KERNEL,
    )(factor, panel, mine, basis)


def merge_kernel(blocks_ref, noise_ref, out_ref, *, step):
    client = lax.axis_index("client")
    total = jnp.zeros(blocks_ref.shape[1:], jnp.float32)
    for i in range(blocks_ref.shape[0]):
        total = total + blocks_ref[i].astype(jnp.float32)
    rows, half = total.shape
    row = pl.ds(pl.multiple_of(lax.div(client, 2) * rows, rows), rows)
    lane = pl.ds(pl.multiple_of(lax.rem(client, 2) * half, half), half)
    total = total + noise_ref[step, row, lane]
    out_ref[...] = jnp.broadcast_to(total.astype(out_ref.dtype), out_ref.shape)


def merge(blocks, noise, step, copies, dtype):
    return pl.pallas_call(
        functools.partial(merge_kernel, step=step),
        in_specs=[IN_VMEM, IN_VMEM],
        out_specs=IN_VMEM,
        out_shape=jax.ShapeDtypeStruct((copies,) + blocks.shape[1:], dtype),
        compiler_params=KERNEL,
    )(blocks, noise)


def ring_sum(here, flip_there, mirror_there, across_there):
    return (flip_there + mirror_there) + (here + across_there)


def gram_kernel(first_ref, second_ref, *refs, step):
    *rings, noise_ref, panel_ref, gram_ref = refs
    rank = panel_ref.shape[0]
    energy = jnp.sum(first_ref[...] + second_ref[...])
    level = jnp.sqrt(jnp.full((8, 128), energy / rank, jnp.float32))[:1, :1]
    panel = ring_sum(*(ref[...] for ref in rings)) + level * noise_ref[step]
    panel_ref[...] = panel
    gram = lax.dot_general(
        panel,
        panel,
        (((1,), (1,)), ((), ())),
        precision=lax.Precision.HIGHEST,
        preferred_element_type=jnp.float32,
    )
    gram = jnp.concatenate([gram[: rank // 2], gram[rank // 2 :]], axis=1)
    gram_ref[...] = jnp.broadcast_to(gram, gram_ref.shape)


def noisy_gram(energies, rings, noise, step):
    rank, rows = rings[0].shape
    return pl.pallas_call(
        functools.partial(gram_kernel, step=step),
        in_specs=[IN_VMEM] * (3 + len(rings)),
        out_specs=[IN_VMEM, IN_VMEM],
        out_shape=[
            jax.ShapeDtypeStruct((rank, rows), jnp.float32),
            jax.ShapeDtypeStruct((SHARDS, rank // 2, 2 * rank), jnp.float32),
        ],
        compiler_params=KERNEL,
    )(*energies, *rings, noise)


def inverse_factor(gram):
    rank = gram.shape[0]
    groups = rank // 8
    lane = lax.broadcasted_iota(jnp.int32, (8, 2 * rank), 1)
    row = lax.broadcasted_iota(jnp.int32, (8, 2 * rank), 0)

    def spread(tile, r):
        return jnp.broadcast_to(tile[r : r + 1, :], tile.shape)

    work = []
    for g in range(groups):
        right = jnp.concatenate(
            [jnp.zeros((8, rank), jnp.float32), gram[8 * g : 8 * g + 8, :]], axis=1
        )
        work.append(jnp.where(lane == row + 8 * g, 1.0, right))
    for b in range(groups):
        column = [
            [
                jnp.broadcast_to(
                    work[g][:, rank + 8 * b + j : rank + 8 * b + j + 1], (8, 2 * rank)
                )
                for g in range(b, groups)
            ]
            for j in range(8)
        ]
        diagonal = jnp.zeros((8, 2 * rank), jnp.float32)
        for j in range(8):
            pivot = spread(column[j][0], j)
            diagonal = jnp.where(row == j, pivot, diagonal)
            inverse = 1.0 / pivot
            ratio = [c * inverse for c in column[j]]
            ratio[0] = jnp.where(row > j, ratio[0], 0.0)
            for k in range(j + 1, 8):
                top = spread(column[k][0], j)
                column[k] = [c - f * top for c, f in zip(column[k], ratio)]
            top = spread(work[b], j)
            for g in range(b, groups):
                work[g] = work[g] - ratio[g - b] * top
        work[b] = work[b] * (1.0 / jnp.sqrt(diagonal))
    return jnp.concatenate([w[:, :rank] for w in work], axis=0)


def solve_kernel(gram_ref, panel_ref, rounded_ref, *basis_ref):
    gram = gram_ref[0]
    for i in range(1, gram_ref.shape[0]):
        gram = gram + gram_ref[i]
    rank = panel_ref.shape[0]
    gram = jnp.concatenate([gram[:, :rank], gram[:, rank:]], axis=0)
    panel = lax.dot_general(
        inverse_factor(gram),
        panel_ref[...],
        (((1,), (0,)), ((), ())),
        precision=lax.Precision.HIGHEST,
        preferred_element_type=jnp.float32,
    )
    rounded_ref[...] = panel.astype(rounded_ref.dtype)
    for ref in basis_ref:
        ref[...] = math.sqrt(D) * panel


def orthonormal(grams, panel, last):
    shapes = [jax.ShapeDtypeStruct(panel.shape, jnp.bfloat16)]
    if last:
        shapes.append(pltpu.VMEM(panel.shape, jnp.float32))
    return pl.pallas_call(
        solve_kernel,
        in_specs=[IN_VMEM, IN_VMEM],
        out_specs=[IN_VMEM] * len(shapes),
        out_shape=shapes,
        compiler_params=KERNEL,
    )(grams, panel)


def ring_parts(panel, ways):
    return [panel] + [lax.ppermute(panel, ("client", "shard"), pairs) for pairs in ways]


def on_device(delta, start_coeffs, noise_p, noise_q):
    coeffs = start_coeffs.T
    rank, columns = coeffs.shape
    panel_noise = noise_p.transpose(0, 2, 1)
    value_noise = noise_q.transpose(0, 2, 1)

    mine, squares = resident(delta[0])
    first, first_energy = first_panel(coeffs, mine, 0)
    second, second_energy = first_panel(coeffs, mine, 1)
    squares = squares + lax.ppermute(squares, "shard", SHARD_STEPS[0])
    squares = squares + lax.ppermute(squares, "shard", SHARD_STEPS[1])
    squares, first = lax.optimization_barrier((squares, first))
    parts = (first, second)
    energies = (first_energy, second_energy)
    there = lax.ppermute(squares, "shard", SHARD_STEPS[-1])
    panel, factor = clip(squares, there, parts, D * columns)
    for step in range(ITERS):
        last = step + 1 == ITERS
        panel = ring_sum(*ring_parts(panel, CLIENT_ROUNDS[0]))
        rings = ring_parts(panel, CLIENT_ROUNDS[1])
        panel, grams = noisy_gram(energies, rings, panel_noise, step)
        grams = lax.all_to_all(grams, "shard", 0, 0)
        rounded, *basis = orthonormal(grams, panel, last)
        away = value_part(rounded, mine, factor, False, jnp.bfloat16)
        away = lax.ppermute(away, "shard", CORE_SWAP)
        if last:
            home, basis = value_store(rounded, mine, factor, basis[0], jnp.float32)
        else:
            home = value_part(rounded, mine, factor, True, jnp.float32)
        chip = (home + away.astype(jnp.float32)).astype(jnp.bfloat16)
        blocks = chip.reshape(CHIPS_Y * CLIENTS, ROW_GROUP, chip.shape[-1])
        blocks = lax.all_to_all(
            blocks, ("client", "shard"), 0, 0, axis_index_groups=SAME_CORE
        )
        if last:
            value = merge(blocks, value_noise, step, CLIENTS, jnp.bfloat16)
            value = lax.all_to_all(value, "client", 0, 0)
        else:
            same = merge(blocks, value_noise, step, CHIPS_Y * CLIENTS, jnp.bfloat16)
            same = lax.all_to_all(same, ("client", "shard"), 0, 0, axis_index_groups=SAME_CORE)
            same = same.reshape(chip.shape)
            other = lax.ppermute(same, "shard", CORE_SWAP)
            own, own_energy = panel_part(own_panel_kernel, same, mine)
            panel, other_energy = panel_part(whole_panel_kernel, other, mine, factor, own)
            energies = (own_energy, other_energy)
    half = value.shape[-1]
    value = value.reshape(rank // ROW_GROUP, 2, ROW_GROUP, half).transpose(0, 2, 1, 3)
    value = value.reshape(rank, 2 * half).astype(jnp.float32)
    return (basis.T, value.T)


def solution(mesh):
    placed = (P("client", "shard", None), P(), P(None, "shard", None), P(None, "shard", None))
    return jax.shard_map(
        on_device,
        mesh=mesh,
        in_specs=placed,
        out_specs=(P("shard", None), P("shard", None)),
        check_vma=False,
    )
```

```python
import functools
import math

import jax
import jax.numpy as jnp
from jax import lax
from jax.experimental import pallas as pl
from jax.experimental.pallas import tpu as pltpu
from jax.sharding import PartitionSpec as P

D = 4096
ITERS = 2
EPS = 1e-06
CLIP_FRACTION = 0.5

CLIENTS = 16
SHARDS = 8
CHIPS_Y = 4
ROW_GROUP = 8

IN_VMEM = pl.BlockSpec(memory_space=pltpu.VMEM)
TILE = jax.ShapeDtypeStruct((8, 128), jnp.float32)
KERNEL = pltpu.CompilerParams(vmem_limit_bytes=16 << 20)


def client_pairs(even, odd):
    pairs = []
    for client in range(CLIENTS):
        for shard in range(SHARDS):
            flip_x, flip_z = odd if shard % 2 else even
            there = flip_x(client // 4) * 4 + flip_z(client % 4)
            pairs.append((client * SHARDS + shard, there * SHARDS + shard))
    return pairs


def keep(i):
    return i


def flip(i):
    return i ^ 1


def mirror(i):
    return 3 - i


def across(i):
    return (i + 2) % 4


WAYS = (flip, mirror, across)
CLIENT_ROUNDS = (
    [client_pairs((keep, way), (way, keep)) for way in WAYS],
    [client_pairs((way, keep), (keep, way)) for way in WAYS],
)
CORE_SWAP = [(i, i ^ 1) for i in range(8)]
SHARD_STEPS = (
    CORE_SWAP,
    [(y * 2 + c, flip(y) * 2 + c) for y in range(4) for c in range(2)],
    [(y * 2 + c, mirror(y) * 2 + c) for y in range(4) for c in range(2)],
)
SAME_CORE = [
    [
        (g * 2 + h) * SHARDS + 2 * y + c
        for y in range(CHIPS_Y)
        for h in range(2)
        for g in range(CLIENTS // 2)
    ]
    for c in range(2)
]


def energy_of(coeffs):
    wide = coeffs.astype(jnp.float32)
    wide = (wide * wide).reshape(-1, 8, wide.shape[-1]).sum(0)
    total = wide[:, :128]
    for k in range(1, wide.shape[1] // 128):
        total = total + wide[:, k * 128 : (k + 1) * 128]
    return total


def resident_kernel(delta_hbm, delta_ref, squares_ref, sems):
    count = sems.shape[0]
    rows = delta_ref.shape[0] // count

    def copy(i):
        part = pl.ds(i * rows, rows)
        return pltpu.make_async_copy(delta_hbm.at[part, :], delta_ref.at[part, :], sems.at[i])

    for i in range(count):
        copy(i).start()
    total = jnp.zeros((8, 128), jnp.float32)
    for i in range(count):
        copy(i).wait()

        def column(c, total):
            part = delta_ref[pl.ds(i * rows, rows), pl.ds(pl.multiple_of(c * 1024, 1024), 1024)]
            part = part.astype(jnp.float32)
            return total + (part * part).reshape(rows // 8, 8, 1024).sum(0)

        wide = lax.fori_loop(
            0, delta_ref.shape[1] // 1024, column, jnp.zeros((8, 1024), jnp.float32), unroll=2
        )
        for k in range(8):
            total = total + wide[:, k * 128 : (k + 1) * 128]
    squares_ref[...] = total


def resident(mine, chunks=16):
    return pl.pallas_call(
        resident_kernel,
        in_specs=[pl.BlockSpec(memory_space=pltpu.HBM)],
        out_specs=[IN_VMEM, IN_VMEM],
        out_shape=[
            pltpu.VMEM(mine.shape, mine.dtype),
            jax.ShapeDtypeStruct((8, 128), jnp.float32),
        ],
        scratch_shapes=[pltpu.SemaphoreType.DMA((chunks,))],
        compiler_params=KERNEL,
    )(pltpu.with_memory_space_constraint(mine, pltpu.HBM))


def first_panel_kernel(coeffs_ref, delta_ref, panel_ref, *energy_ref, columns, squared):
    start, stop = columns
    panel_ref[...] = lax.dot_general(
        coeffs_ref[:, start:stop],
        delta_ref[:, start:stop],
        (((1,), (1,)), ((), ())),
        preferred_element_type=jnp.float32,
    )
    for ref in energy_ref:
        ref[...] = energy_of(coeffs_ref[:, squared[0] : squared[1]])


def first_panel(coeffs, mine, columns, squared=None):
    shapes = [jax.ShapeDtypeStruct((coeffs.shape[0], mine.shape[0]), jnp.float32)]
    if squared:
        shapes.append(TILE)
    return pl.pallas_call(
        functools.partial(first_panel_kernel, columns=columns, squared=squared),
        in_specs=[IN_VMEM, IN_VMEM],
        out_specs=[IN_VMEM] * len(shapes),
        out_shape=shapes,
        compiler_params=KERNEL,
    )(coeffs, mine)


def clip_kernel(here_ref, there_ref, *refs, count):
    *parts, panel_ref, factor_ref = refs
    total = jnp.sum(here_ref[...] + there_ref[...])
    bound = CLIP_FRACTION * math.sqrt(count)
    factor = jnp.minimum(1.0, bound / jnp.sqrt(jnp.full((8, 128), total + EPS, jnp.float32)))
    panel = parts[0][...]
    for part in parts[1:]:
        panel = panel + part[...]
    panel_ref[...] = panel * factor[:1, :1]
    factor_ref[...] = factor


def clip(here, there, parts, count):
    return pl.pallas_call(
        functools.partial(clip_kernel, count=count),
        in_specs=[IN_VMEM] * (2 + len(parts)),
        out_specs=[IN_VMEM] * 2,
        out_shape=[jax.ShapeDtypeStruct(parts[0].shape, jnp.float32), TILE],
        compiler_params=KERNEL,
    )(here, there, *parts)


def core_parity():
    return lax.rem(lax.axis_index("shard"), 2)


def shard_columns(parity, j, width):
    return pl.ds(pl.multiple_of((2 * j + parity) * width, width), width)


def panel_of(parity, coeffs_ref, delta_ref):
    panel = None
    energy = jnp.zeros((8, 128), jnp.float32)
    for j in range(CHIPS_Y):
        coeffs = jnp.concatenate([coeffs_ref[j, 0], coeffs_ref[j, 1]], axis=1)
        part = lax.dot_general(
            coeffs,
            delta_ref[:, shard_columns(parity, j, coeffs.shape[1])],
            (((1,), (1,)), ((), ())),
            preferred_element_type=jnp.float32,
        )
        panel = part if panel is None else panel + part
        energy = energy + energy_of(coeffs)
    return panel, energy


def own_panel_kernel(coeffs_ref, delta_ref, panel_ref, energy_ref):
    panel_ref[...], energy_ref[...] = panel_of(core_parity(), coeffs_ref, delta_ref)


def whole_panel_kernel(coeffs_ref, delta_ref, factor_ref, own_ref, panel_ref, energy_ref):
    panel, energy_ref[...] = panel_of(1 - core_parity(), coeffs_ref, delta_ref)
    panel_ref[...] = (panel + own_ref[...]) * factor_ref[:1, :1]


def panel_part(kernel, coeffs, mine, *more):
    return pl.pallas_call(
        kernel,
        in_specs=[IN_VMEM] * (2 + len(more)),
        out_specs=[IN_VMEM, IN_VMEM],
        out_shape=[jax.ShapeDtypeStruct((coeffs.shape[2], mine.shape[0]), jnp.float32), TILE],
        compiler_params=KERNEL,
    )(coeffs, mine, *more)


def values_of(parity, factor_ref, panel_ref, delta_ref, out_ref):
    half = out_ref.shape[-1]
    for j in range(CHIPS_Y):
        value = factor_ref[:1, :1] * lax.dot_general(
            panel_ref[...],
            delta_ref[:, shard_columns(parity, j, 2 * half)],
            (((1,), (0,)), ((), ())),
            preferred_element_type=jnp.float32,
        )
        value = value.astype(out_ref.dtype)
        out_ref[j, 0] = value[:, :half]
        out_ref[j, 1] = value[:, half:]


def value_kernel(factor_ref, panel_ref, delta_ref, out_ref, *, own):
    parity = core_parity() if own else 1 - core_parity()
    values_of(parity, factor_ref, panel_ref, delta_ref, out_ref)


def value_store_kernel(factor_ref, panel_ref, delta_ref, basis_ref, out_ref, stored_ref, sem):
    copy = pltpu.make_async_copy(basis_ref, stored_ref, sem)
    copy.start()
    values_of(core_parity(), factor_ref, panel_ref, delta_ref, out_ref)
    copy.wait()


def value_shape(panel, mine, dtype):
    half = mine.shape[1] // (4 * CHIPS_Y)
    return jax.ShapeDtypeStruct((CHIPS_Y, 2, panel.shape[0], half), dtype)


def value_part(panel, mine, factor, own, dtype):
    return pl.pallas_call(
        functools.partial(value_kernel, own=own),
        in_specs=[IN_VMEM, IN_VMEM, IN_VMEM],
        out_specs=IN_VMEM,
        out_shape=value_shape(panel, mine, dtype),
        compiler_params=KERNEL,
    )(factor, panel, mine)


def value_store(panel, mine, factor, basis, dtype):
    return pl.pallas_call(
        value_store_kernel,
        in_specs=[IN_VMEM] * 4,
        out_specs=[IN_VMEM, pl.BlockSpec(memory_space=pltpu.HBM)],
        out_shape=[
            value_shape(panel, mine, dtype),
            jax.ShapeDtypeStruct(basis.shape, basis.dtype),
        ],
        scratch_shapes=[pltpu.SemaphoreType.DMA],
        compiler_params=KERNEL,
    )(factor, panel, mine, basis)


def merge_kernel(blocks_ref, noise_ref, out_ref, *, step):
    client = lax.axis_index("client")
    total = jnp.zeros(blocks_ref.shape[1:], jnp.float32)
    for i in range(blocks_ref.shape[0]):
        total = total + blocks_ref[i].astype(jnp.float32)
    rows, half = total.shape
    row = pl.ds(pl.multiple_of(lax.div(client, 2) * rows, rows), rows)
    lane = pl.ds(pl.multiple_of(lax.rem(client, 2) * half, half), half)
    total = total + noise_ref[step, row, lane]
    out_ref[...] = jnp.broadcast_to(total.astype(out_ref.dtype), out_ref.shape)


def merge(blocks, noise, step, copies, dtype):
    return pl.pallas_call(
        functools.partial(merge_kernel, step=step),
        in_specs=[IN_VMEM, IN_VMEM],
        out_specs=IN_VMEM,
        out_shape=jax.ShapeDtypeStruct((copies,) + blocks.shape[1:], dtype),
        compiler_params=KERNEL,
    )(blocks, noise)


def ring_sum(here, flip_there, mirror_there, across_there):
    return (flip_there + mirror_there) + (here + across_there)


def gram_kernel(first_ref, second_ref, *refs, step):
    *rings, noise_ref, panel_ref, gram_ref = refs
    rank = panel_ref.shape[0]
    energy = jnp.sum(first_ref[...] + second_ref[...])
    level = jnp.sqrt(jnp.full((8, 128), energy / rank, jnp.float32))[:1, :1]
    panel = ring_sum(*(ref[...] for ref in rings)) + level * noise_ref[step]
    panel_ref[...] = panel
    gram = lax.dot_general(
        panel,
        panel,
        (((1,), (1,)), ((), ())),
        precision=lax.Precision.HIGHEST,
        preferred_element_type=jnp.float32,
    )
    gram = jnp.concatenate([gram[: rank // 2], gram[rank // 2 :]], axis=1)
    gram_ref[...] = jnp.broadcast_to(gram, gram_ref.shape)


def noisy_gram(energies, rings, noise, step):
    rank, rows = rings[0].shape
    return pl.pallas_call(
        functools.partial(gram_kernel, step=step),
        in_specs=[IN_VMEM] * (3 + len(rings)),
        out_specs=[IN_VMEM, IN_VMEM],
        out_shape=[
            jax.ShapeDtypeStruct((rank, rows), jnp.float32),
            jax.ShapeDtypeStruct((SHARDS, rank // 2, 2 * rank), jnp.float32),
        ],
        compiler_params=KERNEL,
    )(*energies, *rings, noise)


def inverse_factor(gram):
    rank = gram.shape[0]
    groups = rank // 8
    lane = lax.broadcasted_iota(jnp.int32, (8, 2 * rank), 1)
    row = lax.broadcasted_iota(jnp.int32, (8, 2 * rank), 0)

    def spread(tile, r):
        return jnp.broadcast_to(tile[r : r + 1, :], tile.shape)

    work = []
    for g in range(groups):
        right = jnp.concatenate(
            [jnp.zeros((8, rank), jnp.float32), gram[8 * g : 8 * g + 8, :]], axis=1
        )
        work.append(jnp.where(lane == row + 8 * g, 1.0, right))
    for b in range(groups):
        column = [
            [
                jnp.broadcast_to(
                    work[g][:, rank + 8 * b + j : rank + 8 * b + j + 1], (8, 2 * rank)
                )
                for g in range(b, groups)
            ]
            for j in range(8)
        ]
        diagonal = jnp.zeros((8, 2 * rank), jnp.float32)
        for j in range(8):
            pivot = spread(column[j][0], j)
            diagonal = jnp.where(row == j, pivot, diagonal)
            inverse = 1.0 / pivot
            ratio = [c * inverse for c in column[j]]
            ratio[0] = jnp.where(row > j, ratio[0], 0.0)
            for k in range(j + 1, 8):
                top = spread(column[k][0], j)
                column[k] = [c - f * top for c, f in zip(column[k], ratio)]
            top = spread(work[b], j)
            for g in range(b, groups):
                work[g] = work[g] - ratio[g - b] * top
        work[b] = work[b] * (1.0 / jnp.sqrt(diagonal))
    return jnp.concatenate([w[:, :rank] for w in work], axis=0)


def solve_kernel(gram_ref, panel_ref, rounded_ref, *basis_ref):
    gram = gram_ref[0]
    for i in range(1, gram_ref.shape[0]):
        gram = gram + gram_ref[i]
    rank = panel_ref.shape[0]
    gram = jnp.concatenate([gram[:, :rank], gram[:, rank:]], axis=0)
    panel = lax.dot_general(
        inverse_factor(gram),
        panel_ref[...],
        (((1,), (0,)), ((), ())),
        precision=lax.Precision.HIGHEST,
        preferred_element_type=jnp.float32,
    )
    rounded_ref[...] = panel.astype(rounded_ref.dtype)
    for ref in basis_ref:
        ref[...] = math.sqrt(D) * panel


def orthonormal(grams, panel, last):
    shapes = [jax.ShapeDtypeStruct(panel.shape, jnp.bfloat16)]
    if last:
        shapes.append(pltpu.VMEM(panel.shape, jnp.float32))
    return pl.pallas_call(
        solve_kernel,
        in_specs=[IN_VMEM, IN_VMEM],
        out_specs=[IN_VMEM] * len(shapes),
        out_shape=shapes,
        compiler_params=KERNEL,
    )(grams, panel)


def ring_parts(panel, ways):
    return [panel] + [lax.ppermute(panel, ("client", "shard"), pairs) for pairs in ways]


def on_device(delta, start_coeffs, noise_p, noise_q):
    coeffs = start_coeffs.T
    rank, columns = coeffs.shape
    panel_noise = noise_p.transpose(0, 2, 1)
    value_noise = noise_q.transpose(0, 2, 1)

    mine, squares = resident(delta[0])
    low, high = columns * 2 // 7, columns * 4 // 7
    (first,) = first_panel(coeffs, mine, (0, low))
    second, second_energy = first_panel(coeffs, mine, (low, high), (0, high))
    third, third_energy = first_panel(coeffs, mine, (high, columns), (high, columns))
    squares = squares + lax.ppermute(squares, "shard", SHARD_STEPS[0])
    squares, first = lax.optimization_barrier((squares, first))
    squares = squares + lax.ppermute(squares, "shard", SHARD_STEPS[1])
    squares, second = lax.optimization_barrier((squares, second))
    parts = (first, second, third)
    energies = (second_energy, third_energy)
    there = lax.ppermute(squares, "shard", SHARD_STEPS[-1])
    panel, factor = clip(squares, there, parts, D * columns)
    for step in range(ITERS):
        last = step + 1 == ITERS
        panel = ring_sum(*ring_parts(panel, CLIENT_ROUNDS[0]))
        rings = ring_parts(panel, CLIENT_ROUNDS[1])
        panel, grams = noisy_gram(energies, rings, panel_noise, step)
        grams = lax.all_to_all(grams, "shard", 0, 0)
        rounded, *basis = orthonormal(grams, panel, last)
        away = value_part(rounded, mine, factor, False, jnp.bfloat16)
        away = lax.ppermute(away, "shard", CORE_SWAP)
        if last:
            home, basis = value_store(rounded, mine, factor, basis[0], jnp.float32)
        else:
            home = value_part(rounded, mine, factor, True, jnp.float32)
        chip = (home + away.astype(jnp.float32)).astype(jnp.bfloat16)
        blocks = chip.reshape(CHIPS_Y * CLIENTS, ROW_GROUP, chip.shape[-1])
        blocks = lax.all_to_all(
            blocks, ("client", "shard"), 0, 0, axis_index_groups=SAME_CORE
        )
        if last:
            value = merge(blocks, value_noise, step, CLIENTS, jnp.bfloat16)
            value = lax.all_to_all(value, "client", 0, 0)
        else:
            same = merge(blocks, value_noise, step, CHIPS_Y * CLIENTS, jnp.bfloat16)
            same = lax.all_to_all(same, ("client", "shard"), 0, 0, axis_index_groups=SAME_CORE)
            same = same.reshape(chip.shape)
            other = lax.ppermute(same, "shard", CORE_SWAP)
            own, own_energy = panel_part(own_panel_kernel, same, mine)
            panel, other_energy = panel_part(whole_panel_kernel, other, mine, factor, own)
            energies = (own_energy, other_energy)
    half = value.shape[-1]
    value = value.reshape(rank // ROW_GROUP, 2, ROW_GROUP, half).transpose(0, 2, 1, 3)
    value = value.reshape(rank, 2 * half).astype(jnp.float32)
    return (basis.T, value.T)


def solution(mesh):
    placed = (P("client", "shard", None), P(), P(None, "shard", None), P(None, "shard", None))
    return jax.shard_map(
        on_device,
        mesh=mesh,
        in_specs=placed,
        out_specs=(P("shard", None), P("shard", None)),
        check_vma=False,
    )
```
